512 devices in a mesh: stream: 32 (over z, core), xsec: 16 (over y, x).
Axes of the slice: x: 4, y: 4, z: 16, core: 2. Of those that a mesh axis runs over, the one named last changes fastest.
Arguments:
- right_sides: float32 [32, 2048, 2048], P('stream', None, 'xsec'), may hold values from -6 to 6
- lower_first: bfloat16 [32, 2048, 2048], P('stream', None, 'xsec'), may hold values from -0.0625 to 0.0625
- upper_first: bfloat16 [32, 2048, 2048], P('stream', None, 'xsec'), may hold values from -0.0625 to 0.0625
- lower_second: bfloat16 [32, 2048, 2048], P('stream', None, 'xsec'), may hold values from -0.0625 to 0.0625
- upper_second: bfloat16 [32, 2048, 2048], P('stream', None, 'xsec'), may hold values from -0.0625 to 0.0625
Outputs:
- reduced: float32 [32, 2048, 2048], P('stream', None, 'xsec')
The draws below stay inside these ranges and needn't reach their ends.
All inputs are finite; a program needn't handle non-finite values.
Results may differ from the reference program's by a relative error of at most 0.0023.
Values may be sent and summed in bfloat16 or wider, within the bound.
No kernel may reach another device: no remote copies, remote signals or barrier semaphores. Data moves between devices by JAX's collectives and lax.ppermute only.
A program may use at most 128 MiB of HBM per device.

```python
import jax
import jax.numpy as jnp
from jax import lax

M = 2048
R = 2048
IFACE = 32


def steps_of(rng, extent, cuts, smallest, largest):
    loudness = 1.0
    for position, parts in cuts:
        draws = jax.random.uniform(jax.random.fold_in(jax.random.fold_in(rng, 6), position), (parts,), jnp.float32, smallest / len(cuts), largest / len(cuts))
        loudness = loudness * jnp.repeat(jnp.exp(draws), extent[position] // parts).reshape((-1,) + (1,) * (len(extent) - 1 - position))
    return loudness


def scatter_about(stream_key, dims, width, limit, split=(), held_as=jnp.bfloat16):
    result = jax.random.normal(stream_key, dims, jnp.float32) * width
    if len(split) > 0:
        result = steps_of(stream_key, dims, split, -0.22, 0.18) * result
    return jnp.clip(result, min=-limit, max=limit).astype(held_as)


def setup_inputs(seed: int = 0) -> dict:
    key_list = jax.random.split(jax.random.key(seed), 6)
    right_sides = scatter_about(key_list[0], (IFACE, M, R), 1.0, 6.0, ((0, 32), (2, 16)), jnp.float32)
    lower_first = scatter_about(key_list[1], (IFACE, M, M), (4 * M) ** -0.5, 0.0625, ((0, 32), (2, 16)))
    upper_first = scatter_about(key_list[2], (IFACE, M, M), (4 * M) ** -0.5, 0.0625, ((0, 32), (2, 16)))
    lower_second = scatter_about(key_list[3], (IFACE, M, M), (4 * M) ** -0.5, 0.0625, ((0, 32), (2, 16)))
    upper_second = scatter_about(key_list[4], (IFACE, M, M), (4 * M) ** -0.5, 0.0625, ((0, 32), (2, 16)))
    return dict(right_sides=right_sides, lower_first=lower_first, upper_first=upper_first, lower_second=lower_second, upper_second=upper_second)


def shifted(sent, distance):
    padding = jnp.zeros((distance,) + sent.shape[1:], sent.dtype)
    from_below = jnp.concatenate([padding, sent[:-distance]], axis=0)
    from_above = jnp.concatenate([sent[distance:], padding], axis=0)
    return from_below, from_above


def coupled(blocks_in):
    lower_block, upper_block, from_below, from_above = blocks_in
    first_term = jnp.dot(lower_block.astype(jnp.float32), from_below.astype(jnp.float32), precision=lax.Precision.HIGHEST)
    second_term = jnp.dot(upper_block.astype(jnp.float32), from_above.astype(jnp.float32), precision=lax.Precision.HIGHEST)
    return first_term + second_term


def reduce_level(field, lower_blocks, upper_blocks, distance):
    sent = field.astype(jnp.bfloat16)
    from_below, from_above = shifted(sent, distance)
    return field + lax.map(coupled, (lower_blocks, upper_blocks, from_below, from_above))


def reference(right_sides, lower_first, upper_first, lower_second, upper_second):
    level_one = reduce_level(right_sides, lower_first, upper_first, 1)
    return reduce_level(level_one, lower_second, upper_second, 2)
```

```python
import jax
import jax.numpy as jnp
from jax import lax
from jax.experimental import pallas as pl
from jax.experimental.pallas import tpu as pltpu
from jax.sharding import Mesh, PartitionSpec as P

Z, CORES, Y, X = 16, 2, 4, 4
PLANES = Z * CORES
M = 2048
BLK = M // Y
COL = 128
AXES = ("z", "core", "y", "x")


def device_index(plane, y, x):
    return (plane * Y + y) * X + x


def moved(value, planes, ys):
    pairs = []
    for plane in range(PLANES):
        if not 0 <= plane + planes < PLANES:
            continue
        for y in range(Y):
            for x in range(X):
                pairs.append(
                    (
                        device_index(plane, y, x),
                        device_index(plane + planes, (y + ys) % Y, x),
                    )
                )
    return lax.ppermute(value, AXES, pairs)


def first_kernel(y_ref, a_ref, *refs):
    below, above = refs[0:4], refs[4:8]
    rhs_ref, corr_ref, sent_ref, acc_ref = refs[8:]
    step = pl.program_id(0)

    @pl.when(step == 0)
    def _():
        acc_ref[...] = jnp.zeros_like(acc_ref)

    total = acc_ref[...]
    for which, parts in ((0, below), (1, above)):
        left = jnp.concatenate([a_ref[x, 0, which] for x in range(X)], axis=1)
        right = jnp.concatenate([part[...] for part in parts], axis=1)
        total = total + jnp.dot(left, right, preferred_element_type=jnp.float32)
    acc_ref[...] = total

    @pl.when(step == Y - 1)
    def _():
        for d in range(Y):
            piece = acc_ref[:, d * COL : (d + 1) * COL]
            corr_ref[d] = piece
            owner = lax.rem(y_ref[0] + d, Y)
            sent_ref[d] = (rhs_ref[owner] + piece).astype(jnp.bfloat16)


def first_level(y, blocks, below, above, rhs):
    part = pl.BlockSpec((BLK, COL), lambda k, y: (k, 0))
    whole = pl.BlockSpec((Y, BLK, COL), lambda k, y: (0, 0, 0))
    return pl.pallas_call(
        first_kernel,
        name="first_level",
        out_shape=(
            jax.ShapeDtypeStruct((Y, BLK, COL), jnp.float32),
            jax.ShapeDtypeStruct((Y, BLK, COL), jnp.bfloat16),
        ),
        grid_spec=pltpu.PrefetchScalarGridSpec(
            num_scalar_prefetch=1,
            grid=(Y,),
            in_specs=[
                pl.BlockSpec((X, 1, 2, BLK, COL), lambda k, y: (0, k, 0, 0, 0))
            ]
            + [part] * 8
            + [whole],
            out_specs=(whole, whole),
            scratch_shapes=[pltpu.VMEM((BLK, Y * COL), jnp.float32)],
        ),
        compiler_params=pltpu.CompilerParams(vmem_limit_bytes=40 << 20),
        cost_estimate=pl.CostEstimate(
            flops=4 * BLK * M * Y * COL, bytes_accessed=11 << 20, transcendentals=0
        ),
    )(y, blocks, *below, *above, rhs)


def second_kernel(
    y_ref, lo_ref, up_ref, below, above, corr_ref, rhs_ref, own_ref, *outs
):
    step = pl.program_id(0)
    total = None
    for a_ref, b_ref in ((lo_ref, below), (up_ref, above)):
        left = jnp.concatenate([a_ref[x] for x in range(X)], axis=1)
        right = jnp.concatenate([b_ref[d] for d in range(Y)], axis=1)
        term = jnp.dot(left, right, preferred_element_type=jnp.float32)
        total = term if total is None else total + term
    here = step == y_ref[0]
    for d in range(Y):
        piece = total[:, d * COL : (d + 1) * COL]
        piece = piece + jnp.where(here, corr_ref[d], 0.0)
        if d == 0:
            own_ref[...] = piece + rhs_ref[...]
        else:
            outs[d - 1][...] = piece.astype(jnp.bfloat16)


def second_level(y, lo, up, below, above, corr, rhs):
    rows = pl.BlockSpec((BLK, COL), lambda m, y: (m, 0))
    blocks = pl.BlockSpec((X, BLK, COL), lambda m, y: (0, m, 0))
    whole = pl.BlockSpec((Y, BLK, COL), lambda m, y: (0, 0, 0))
    return pl.pallas_call(
        second_kernel,
        name="second_level",
        out_shape=(jax.ShapeDtypeStruct((M, COL), jnp.float32),)
        + (jax.ShapeDtypeStruct((M, COL), jnp.bfloat16),) * 3,
        grid_spec=pltpu.PrefetchScalarGridSpec(
            num_scalar_prefetch=1,
            grid=(Y,),
            in_specs=[blocks, blocks, whole, whole, whole, rows],
            out_specs=(rows,) * 4,
        ),
        compiler_params=pltpu.CompilerParams(vmem_limit_bytes=40 << 20),
        cost_estimate=pl.CostEstimate(
            flops=4 * BLK * M * Y * COL, bytes_accessed=9 << 20, transcendentals=0
        ),
    )(y, lo, up, below, above, corr, rhs)


def on_device(right_sides, lower_first, upper_first, lower_second, upper_second):
    rhs = right_sides[0]
    y = lax.axis_index("y").astype(jnp.int32)[None]

    lo_two = lax.all_gather(lower_second[0], "x", axis=0)

    sent_one = rhs.astype(jnp.bfloat16)
    own = [sent_one] + [moved(sent_one, 0, -d) for d in range(1, Y)]

    firsts = jnp.stack(
        [lower_first[0].reshape(Y, BLK, COL), upper_first[0].reshape(Y, BLK, COL)],
        axis=1,
    )
    firsts = lax.all_to_all(firsts, "y", 0, 0, tiled=True)
    blocks = lax.all_gather(firsts, "x", axis=0)

    below = [moved(part, 1, 0) for part in own]
    above = [moved(part, -1, 0) for part in own]
    rhs_rows = lax.all_to_all(rhs.reshape(Y, BLK, COL), "y", 0, 0, tiled=True)

    upper, blocks = lax.optimization_barrier((upper_second[0], blocks))
    up_two = lax.all_gather(upper, "x", axis=0)

    corr, sent_two = first_level(y, blocks, below, above, rhs_rows)
    below_two = moved(sent_two, 2, 0)
    above_two = moved(sent_two, -2, 0)
    total, *parts = second_level(y, lo_two, up_two, below_two, above_two, corr, rhs)
    for d in range(1, Y):
        total = total + moved(parts[d - 1], 0, d).astype(jnp.float32)
    return total[None]


def solution(mesh):
    fine = Mesh(mesh.devices.reshape(Z, CORES, Y, X), AXES)
    spec = P(("z", "core"), None, ("y", "x"))
    return jax.shard_map(
        on_device,
        mesh=fine,
        in_specs=(spec,) * 5,
        out_specs=spec,
        check_vma=False,
    )
```

```python
import jax
import jax.numpy as jnp
from jax import lax
from jax.experimental import pallas as pl
from jax.experimental.pallas import tpu as pltpu
from jax.sharding import Mesh, PartitionSpec as P

Z, CORES, Y, X = 16, 2, 4, 4
PLANES = Z * CORES
M = 2048
BLK = M // Y
COL = 128
AXES = ("z", "core", "y", "x")


def device_index(plane, y, x):
    return (plane * Y + y) * X + x


def moved(value, planes=0, ys=0, xs=0):
    pairs = []
    for plane in range(PLANES):
        if not 0 <= plane + planes < PLANES:
            continue
        for y in range(Y):
            for x in range(X):
                target = device_index(plane + planes, (y + ys) % Y, (x + xs) % X)
                pairs.append((device_index(plane, y, x), target))
    return lax.ppermute(value, AXES, pairs)


def after(value, *before):
    return lax.optimization_barrier((value,) + before)[0]


def rows_in_order(at_ref, ref, row):
    return [
        ref[row + (pl.ds(pl.multiple_of(lax.rem(at_ref[1] + e, X) * COL, COL), COL),)]
        for e in range(X)
    ]


def first_kernel(at_ref, *refs):
    lower, upper = refs[0:4], refs[4:8]
    below, above = refs[8:12], refs[12:16]
    rhs_ref, corr_ref, sent_ref, acc_ref = refs[16:]
    step = pl.program_id(0)

    @pl.when(step == 0)
    def _():
        acc_ref[...] = jnp.zeros_like(acc_ref)

    total = acc_ref[...]
    for blocks, parts in ((lower, below), (upper, above)):
        left = jnp.concatenate([block[0] for block in blocks], axis=1)
        right = [
            jnp.concatenate(rows_in_order(at_ref, part, ()), axis=0) for part in parts
        ]
        right = jnp.concatenate(right, axis=1)
        total = total + jnp.dot(left, right, preferred_element_type=jnp.float32)
    acc_ref[...] = total

    @pl.when(step == Y - 1)
    def _():
        for d in range(Y):
            piece = acc_ref[:, d * COL : (d + 1) * COL]
            corr_ref[d] = piece
            owner = lax.rem(at_ref[0] + d, Y)
            sent_ref[d] = (rhs_ref[owner] + piece).astype(jnp.bfloat16)


def first_level(at, lower, upper, below, above, rhs):
    block = pl.BlockSpec((1, BLK, COL), lambda k, at: (k, 0, 0))
    part = pl.BlockSpec((BLK, COL), lambda k, at: (k, 0))
    whole = pl.BlockSpec((Y, BLK, COL), lambda k, at: (0, 0, 0))
    return pl.pallas_call(
        first_kernel,
        name="first_level",
        out_shape=(
            jax.ShapeDtypeStruct((Y, BLK, COL), jnp.float32),
            jax.ShapeDtypeStruct((Y, BLK, COL), jnp.bfloat16),
        ),
        grid_spec=pltpu.PrefetchScalarGridSpec(
            num_scalar_prefetch=1,
            grid=(Y,),
            in_specs=[block] * 8 + [part] * 8 + [whole],
            out_specs=(whole, whole),
            scratch_shapes=[pltpu.VMEM((BLK, Y * COL), jnp.float32)],
        ),
        compiler_params=pltpu.CompilerParams(vmem_limit_bytes=20 << 20),
        cost_estimate=pl.CostEstimate(
            flops=4 * BLK * M * Y * COL, bytes_accessed=11 << 20, transcendentals=0
        ),
    )(at, *lower, *upper, *below, *above, rhs)


def second_kernel(at_ref, *refs):
    lower, upper = refs[0:4], refs[4:8]
    below, above, corr_ref, rhs_ref, own_ref, *outs = refs[8:]
    step = pl.program_id(0)
    total = None
    for blocks, b_ref in ((lower, below), (upper, above)):
        left = jnp.concatenate([block[...] for block in blocks], axis=1)
        right = [
            jnp.concatenate(rows_in_order(at_ref, b_ref, (d,)), axis=0)
            for d in range(Y)
        ]
        right = jnp.concatenate(right, axis=1)
        term = jnp.dot(left, right, preferred_element_type=jnp.float32)
        total = term if total is None else total + term
    here = step == at_ref[0]
    for d in range(Y):
        piece = total[:, d * COL : (d + 1) * COL]
        piece = piece + jnp.where(here, corr_ref[d], 0.0)
        if d == 0:
            own_ref[...] = piece + rhs_ref[...]
        else:
            outs[d - 1][...] = piece.astype(jnp.bfloat16)


def second_level(at, lower, upper, below, above, corr, rhs):
    rows = pl.BlockSpec((BLK, COL), lambda m, at: (m, 0))
    whole = pl.BlockSpec((Y, BLK, COL), lambda m, at: (0, 0, 0))
    return pl.pallas_call(
        second_kernel,
        name="second_level",
        out_shape=(jax.ShapeDtypeStruct((M, COL), jnp.float32),)
        + (jax.ShapeDtypeStruct((M, COL), jnp.bfloat16),) * 3,
        grid_spec=pltpu.PrefetchScalarGridSpec(
            num_scalar_prefetch=1,
            grid=(Y,),
            in_specs=[rows] * 8 + [whole, whole, whole, rows],
            out_specs=(rows,) * 4,
        ),
        compiler_params=pltpu.CompilerParams(vmem_limit_bytes=20 << 20),
        cost_estimate=pl.CostEstimate(
            flops=4 * BLK * M * Y * COL, bytes_accessed=9 << 20, transcendentals=0
        ),
    )(at, *lower, *upper, below, above, corr, rhs)


def on_device(right_sides, lower_first, upper_first, lower_second, upper_second):
    rhs = right_sides[0]
    at = jnp.stack([lax.axis_index("y"), lax.axis_index("x")]).astype(jnp.int32)

    def exchanged(value):
        return lax.all_to_all(value.reshape(Y, BLK, COL), "y", 0, 0, tiled=True)

    lo, up = exchanged(lower_first[0]), exchanged(upper_first[0])
    lo_two, up_two = lower_second[0], upper_second[0]
    lo_two_left, lo_two_right = moved(lo_two, xs=1), moved(lo_two, xs=-1)

    sent_one = rhs.astype(jnp.bfloat16)
    below, above = [moved(sent_one, 1)], [moved(sent_one, -1)]

    lo_left, lo_right = moved(lo, xs=1), moved(lo, xs=-1)
    up_left, up_right = moved(up, xs=1), moved(up, xs=-1)
    late = after(sent_one, up)
    for d in range(1, Y):
        part = moved(late, ys=-d)
        below.append(moved(part, 1))
        above.append(moved(part, -1))
    lo_far, up_far = moved(lo_left, xs=1), moved(up_right, xs=-1)
    rhs_rows = exchanged(after(rhs, up))

    up_two_in = after(up_two, lo_left, up_right)
    up_two_left, up_two_right = moved(up_two_in, xs=1), moved(up_two_in, xs=-1)
    lo_two_far = moved(after(lo_two_left, lo_far), xs=1)
    up_two_far = moved(up_two_right, xs=-1)

    corr, sent_two = first_level(
        at,
        (lo, lo_right, lo_far, lo_left),
        (up, up_right, up_far, up_left),
        below,
        above,
        rhs_rows,
    )
    below_two, above_two = moved(sent_two, 2), moved(sent_two, -2)
    total, *parts = second_level(
        at,
        (lo_two, lo_two_right, lo_two_far, lo_two_left),
        (up_two, up_two_right, up_two_far, up_two_left),
        below_two,
        above_two,
        corr,
        rhs,
    )
    for d in range(1, Y):
        total = total + moved(parts[d - 1], ys=d).astype(jnp.float32)
    return total[None]


def solution(mesh):
    fine = Mesh(mesh.devices.reshape(Z, CORES, Y, X), AXES)
    spec = P(("z", "core"), None, ("y", "x"))
    return jax.shard_map(
        on_device,
        mesh=fine,
        in_specs=(spec,) * 5,
        out_specs=spec,
        check_vma=False,
    )
```

```python
import jax
import jax.numpy as jnp
from jax import lax
from jax.experimental import pallas as pl
from jax.experimental.pallas import tpu as pltpu
from jax.sharding import Mesh, PartitionSpec as P

Z, CORES, Y, X = 16, 2, 4, 4
PLANES = Z * CORES
M = 2048
BLK = M // Y
COL = 128
AXES = ("z", "core", "y", "x")


def device_index(plane, y, x):
    return (plane * Y + y) * X + x


def moved(value, planes=0, ys=0, xs=0):
    pairs = []
    for plane in range(PLANES):
        if not 0 <= plane + planes < PLANES:
            continue
        for y in range(Y):
            for x in range(X):
                target = device_index(plane + planes, (y + ys) % Y, (x + xs) % X)
                pairs.append((device_index(plane, y, x), target))
    return lax.ppermute(value, AXES, pairs)


def after(value, *before):
    return lax.optimization_barrier((value,) + before)[0]


def rows_in_order(at_ref, ref, row):
    return [
        ref[row + (pl.ds(pl.multiple_of(lax.rem(at_ref[1] + e, X) * COL, COL), COL),)]
        for e in range(X)
    ]


def first_kernel(
    at_ref,
    own_ref,
    left_ref,
    right_ref,
    a_far_ref,
    b_far_ref,
    near_ref,
    down_ref,
    up_ref,
    below_far_ref,
    above_far_ref,
    rhs_ref,
    corr_ref,
    sent_ref,
    acc_ref,
):
    step = pl.program_id(0)

    @pl.when(step == 0)
    def _():
        acc_ref[...] = jnp.zeros_like(acc_ref)

    total = acc_ref[...]
    for side, far_ref in ((0, below_far_ref), (1, above_far_ref)):
        blocks = [
            own_ref[0, side],
            right_ref[0, side],
            jnp.where(step < Y // 2, a_far_ref[0, side], b_far_ref[0, side]),
            left_ref[0, side],
        ]
        left = jnp.concatenate(blocks, axis=1)
        parts = (
            (near_ref, (side,)),
            (up_ref, (side,)),
            (far_ref, ()),
            (down_ref, (side,)),
        )
        right = [
            jnp.concatenate(rows_in_order(at_ref, part, row), axis=0)
            for part, row in parts
        ]
        right = jnp.concatenate(right, axis=1)
        total = total + jnp.dot(left, right, preferred_element_type=jnp.float32)
    acc_ref[...] = total

    @pl.when(step == Y - 1)
    def _():
        for d in range(Y):
            piece = acc_ref[:, d * COL : (d + 1) * COL]
            corr_ref[d] = piece
            owner = lax.rem(at_ref[0] + d, Y)
            sent_ref[d] = (rhs_ref[owner] + piece).astype(jnp.bfloat16)


def first_level(at, pair, left, right, a_far, b_far, near, down, up, below, above, rhs):
    half = Y // 2
    blocks = pl.BlockSpec((1, 2, BLK, COL), lambda k, at: (k, 0, 0, 0))
    a_blocks = pl.BlockSpec(
        (1, 2, BLK, COL), lambda k, at: (jnp.minimum(k, half - 1), 0, 0, 0)
    )
    b_blocks = pl.BlockSpec(
        (1, 2, BLK, COL), lambda k, at: (jnp.maximum(k - half, 0), 0, 0, 0)
    )
    parts = pl.BlockSpec((2, BLK, COL), lambda k, at: (0, k, 0))
    part = pl.BlockSpec((BLK, COL), lambda k, at: (k, 0))
    whole = pl.BlockSpec((Y, BLK, COL), lambda k, at: (0, 0, 0))
    return pl.pallas_call(
        first_kernel,
        name="first_level",
        out_shape=(
            jax.ShapeDtypeStruct((Y, BLK, COL), jnp.float32),
            jax.ShapeDtypeStruct((Y, BLK, COL), jnp.bfloat16),
        ),
        grid_spec=pltpu.PrefetchScalarGridSpec(
            num_scalar_prefetch=1,
            grid=(Y,),
            in_specs=[blocks] * 3
            + [a_blocks, b_blocks]
            + [parts] * 3
            + [part] * 2
            + [whole],
            out_specs=(whole, whole),
            scratch_shapes=[pltpu.VMEM((BLK, Y * COL), jnp.float32)],
        ),
        compiler_params=pltpu.CompilerParams(vmem_limit_bytes=32 << 20),
        cost_estimate=pl.CostEstimate(
            flops=4 * BLK * M * Y * COL, bytes_accessed=11 << 20, transcendentals=0
        ),
    )(at, pair, left, right, a_far, b_far, near, down, up, below, above, rhs)


def second_kernel(
    at_ref, a_ref, below, above, corr_ref, rhs_ref, own_ref, *outs
):
    step = pl.program_id(0)
    total = None
    for side, b_ref in ((0, below), (1, above)):
        left = jnp.concatenate([a_ref[x, side] for x in range(X)], axis=1)
        right = jnp.concatenate([b_ref[d] for d in range(Y)], axis=1)
        term = jnp.dot(left, right, preferred_element_type=jnp.float32)
        total = term if total is None else total + term
    here = step == at_ref[0]
    for d in range(Y):
        piece = total[:, d * COL : (d + 1) * COL]
        piece = piece + jnp.where(here, corr_ref[d], 0.0)
        if d == 0:
            own_ref[...] = piece + rhs_ref[...]
        else:
            outs[d - 1][...] = piece.astype(jnp.bfloat16)


def second_level(at, blocks, below, above, corr, rhs):
    rows = pl.BlockSpec((BLK, COL), lambda m, at: (m, 0))
    pairs = pl.BlockSpec((X, 2, BLK, COL), lambda m, at: (0, 0, m, 0))
    whole = pl.BlockSpec((Y, BLK, COL), lambda m, at: (0, 0, 0))
    return pl.pallas_call(
        second_kernel,
        name="second_level",
        out_shape=(jax.ShapeDtypeStruct((M, COL), jnp.float32),)
        + (jax.ShapeDtypeStruct((M, COL), jnp.bfloat16),) * 3,
        grid_spec=pltpu.PrefetchScalarGridSpec(
            num_scalar_prefetch=1,
            grid=(Y,),
            in_specs=[pairs, whole, whole, whole, rows],
            out_specs=(rows,) * 4,
        ),
        compiler_params=pltpu.CompilerParams(vmem_limit_bytes=56 << 20),
        cost_estimate=pl.CostEstimate(
            flops=4 * BLK * M * Y * COL, bytes_accessed=9 << 20, transcendentals=0
        ),
    )(at, blocks, below, above, corr, rhs)


def relayed(pair, halves, **axis):
    name = "xs" if axis["over"] == "x" else "ys"
    left, right = moved(pair, **{name: 1}), moved(pair, **{name: -1})
    first, second = halves
    far = moved(first(left), **{name: 1}), moved(second(right), **{name: -1})
    return (left, right) + far


def on_device(right_sides, lower_first, upper_first, lower_second, upper_second):
    rhs = right_sides[0]
    at = jnp.stack([lax.axis_index("y"), lax.axis_index("x")]).astype(jnp.int32)
    halves = (lambda v: v[: Y // 2], lambda v: v[Y // 2 :])
    sides = (lambda v: v[0], lambda v: v[1])

    def exchanged(value):
        return lax.all_to_all(value, "y", 0, 0, tiled=True)

    seconds = jnp.stack([lower_second[0], upper_second[0]])
    seconds = lax.all_gather(seconds, "x", axis=0)

    firsts = [v[0].reshape(Y, BLK, COL) for v in (lower_first, upper_first)]
    firsts = jnp.stack(firsts, axis=1)
    sent_one = after(rhs, firsts).astype(jnp.bfloat16)
    pair = exchanged(firsts)
    near = after(jnp.stack([moved(sent_one, 1), moved(sent_one, -1)]), pair)

    left, right, a_far, b_far = relayed(pair, halves, over="x")
    down, up, below_far, above_far = relayed(near, sides, over="y")
    rhs_rows = exchanged(after(rhs, pair).reshape(Y, BLK, COL))

    corr, sent_two = first_level(
        at,
        pair,
        left,
        right,
        a_far,
        b_far,
        near,
        down,
        up,
        below_far,
        above_far,
        rhs_rows,
    )
    below_two, above_two = moved(sent_two, 2), moved(sent_two, -2)
    total, *parts = second_level(at, seconds, below_two, above_two, corr, rhs)
    for d in range(1, Y):
        total = total + moved(parts[d - 1], ys=d).astype(jnp.float32)
    return total[None]


def solution(mesh):
    fine = Mesh(mesh.devices.reshape(Z, CORES, Y, X), AXES)
    spec = P(("z", "core"), None, ("y", "x"))
    return jax.shard_map(
        on_device,
        mesh=fine,
        in_specs=(spec,) * 5,
        out_specs=spec,
        check_vma=False,
    )
```

```python
import functools

import jax
import jax.numpy as jnp
from jax import lax
from jax.experimental import pallas as pl
from jax.experimental.pallas import tpu as pltpu
from jax.sharding import Mesh, PartitionSpec as P

Z, CORES, Y, X = 16, 2, 4, 4
PLANES = Z * CORES
M = 2048
BLK = M // Y
COL = 128
AXES = ("z", "core", "y", "x")


def device_index(plane, y, x):
    return (plane * Y + y) * X + x


def moved(value, planes=0, ys=0, xs=0):
    pairs = []
    for plane in range(PLANES):
        if not 0 <= plane + planes < PLANES:
            continue
        for y in range(Y):
            for x in range(X):
                target = device_index(plane + planes, (y + ys) % Y, (x + xs) % X)
                pairs.append((device_index(plane, y, x), target))
    return lax.ppermute(value, AXES, pairs)


def after(value, *before):
    return lax.optimization_barrier((value,) + before)[0]


def rows_in_order(at_ref, ref, row):
    return [
        ref[row + (pl.ds(pl.multiple_of(lax.rem(at_ref[1] + e, X) * COL, COL), COL),)]
        for e in range(X)
    ]


FIRST_GROUPS, LAST_GROUPS = (2, 1), (3, 0)


def first_kernel(
    groups,
    at_ref,
    own_ref,
    left_ref,
    right_ref,
    far_ref,
    near_ref,
    down_ref,
    up_ref,
    below_far_ref,
    above_far_ref,
    rhs_ref,
    corr_ref,
    sent_ref,
    acc_ref,
):
    step = pl.program_id(0)

    @pl.when(step == 0)
    def _():
        acc_ref[...] = jnp.zeros_like(acc_ref)

    total = acc_ref[...]
    for side, b_far_ref in ((0, below_far_ref), (1, above_far_ref)):
        blocks = (own_ref, right_ref, far_ref, left_ref)
        left = jnp.concatenate([block[0, side] for block in blocks], axis=1)
        parts = (
            (near_ref, (side,)),
            (up_ref, (side,)),
            (b_far_ref, ()),
            (down_ref, (side,)),
        )
        right = [
            jnp.concatenate(rows_in_order(at_ref, *parts[d]), axis=0) for d in groups
        ]
        right = jnp.concatenate(right, axis=1)
        total = total + jnp.dot(left, right, preferred_element_type=jnp.float32)
    acc_ref[...] = total

    @pl.when(step == Y - 1)
    def _():
        for i, d in enumerate(groups):
            piece = acc_ref[:, i * COL : (i + 1) * COL]
            corr_ref[i] = piece
            owner = lax.rem(at_ref[0] + d, Y)
            sent_ref[i] = (rhs_ref[owner] + piece).astype(jnp.bfloat16)


def first_level(groups, at, blocks, parts, rhs):
    count = len(groups)
    block = pl.BlockSpec((1, 2, BLK, COL), lambda k, at: (k, 0, 0, 0))
    both = pl.BlockSpec((2, BLK, COL), lambda k, at: (0, k, 0))
    part = pl.BlockSpec((BLK, COL), lambda k, at: (k, 0))
    whole = pl.BlockSpec((Y, BLK, COL), lambda k, at: (0, 0, 0))
    out = pl.BlockSpec((count, BLK, COL), lambda k, at: (0, 0, 0))
    return pl.pallas_call(
        functools.partial(first_kernel, groups),
        name="first_level",
        out_shape=(
            jax.ShapeDtypeStruct((count, BLK, COL), jnp.float32),
            jax.ShapeDtypeStruct((count, BLK, COL), jnp.bfloat16),
        ),
        grid_spec=pltpu.PrefetchScalarGridSpec(
            num_scalar_prefetch=1,
            grid=(Y,),
            in_specs=[block] * 4 + [both] * 3 + [part] * 2 + [whole],
            out_specs=(out, out),
            scratch_shapes=[pltpu.VMEM((BLK, count * COL), jnp.float32)],
        ),
        compiler_params=pltpu.CompilerParams(vmem_limit_bytes=32 << 20),
        cost_estimate=pl.CostEstimate(
            flops=4 * BLK * M * count * COL,
            bytes_accessed=9 << 20,
            transcendentals=0,
        ),
    )(at, *blocks, *parts, rhs)


def second_kernel(
    groups,
    at_ref,
    lo_ref,
    up_ref,
    left_ref,
    right_ref,
    lo_far_ref,
    up_far_ref,
    below,
    above,
    corr_ref,
    rhs_ref,
    *outs,
):
    step = pl.program_id(0)
    lower = [lo_ref[...], right_ref[0], lo_far_ref[...], left_ref[0]]
    upper = [up_ref[...], right_ref[1], up_far_ref[...], left_ref[1]]
    total = None
    for blocks, b_ref in ((lower, below), (upper, above)):
        left = jnp.concatenate(blocks, axis=1)
        right = [
            jnp.concatenate(rows_in_order(at_ref, b_ref, (i,)), axis=0)
            for i in range(len(groups))
        ]
        right = jnp.concatenate(right, axis=1)
        term = jnp.dot(left, right, preferred_element_type=jnp.float32)
        total = term if total is None else total + term
    here = step == at_ref[0]
    for i, d in enumerate(groups):
        piece = total[:, i * COL : (i + 1) * COL]
        piece = piece + jnp.where(here, corr_ref[i], 0.0)
        if d == 0:
            piece = piece + rhs_ref[...]
        outs[i][...] = piece.astype(outs[i].dtype)


def second_level(groups, at, blocks, below, above, corr, rhs):
    count = len(groups)
    rows = pl.BlockSpec((BLK, COL), lambda m, at: (m, 0))
    pair = pl.BlockSpec((2, BLK, COL), lambda m, at: (0, m, 0))
    whole = pl.BlockSpec((count, BLK, COL), lambda m, at: (0, 0, 0))
    return pl.pallas_call(
        functools.partial(second_kernel, groups),
        name="second_level",
        out_shape=tuple(
            jax.ShapeDtypeStruct((M, COL), jnp.bfloat16 if d else jnp.float32)
            for d in groups
        ),
        grid_spec=pltpu.PrefetchScalarGridSpec(
            num_scalar_prefetch=1,
            grid=(Y,),
            in_specs=[rows, rows, pair, pair, rows, rows, whole, whole, whole, rows],
            out_specs=(rows,) * count,
        ),
        compiler_params=pltpu.CompilerParams(vmem_limit_bytes=32 << 20),
        cost_estimate=pl.CostEstimate(
            flops=4 * BLK * M * count * COL,
            bytes_accessed=6 << 20,
            transcendentals=0,
        ),
    )(at, *blocks, below, above, corr, rhs)


def on_device(right_sides, lower_first, upper_first, lower_second, upper_second):
    rhs = right_sides[0]
    at = jnp.stack([lax.axis_index("y"), lax.axis_index("x")]).astype(jnp.int32)

    def exchanged(value):
        return lax.all_to_all(value, "y", 0, 0, tiled=True)

    firsts = [v[0].reshape(Y, BLK, COL) for v in (lower_first, upper_first)]
    firsts = jnp.stack(firsts, axis=1)
    sent_one = after(rhs, firsts).astype(jnp.bfloat16)
    own = exchanged(firsts)
    near = jnp.stack([moved(sent_one, 1), moved(sent_one, -1)])

    lo_two, up_two = lower_second[0], upper_second[0]
    seconds = after(jnp.stack([lo_two, up_two]), sent_one)
    two_left, two_right = moved(seconds, xs=1), moved(seconds, xs=-1)

    left, right, far = moved(own, xs=1), moved(own, xs=-1), moved(own, xs=2)
    down, up = moved(near, ys=1), moved(near, ys=-1)
    below_far, above_far = moved(down[0], ys=1), moved(up[1], ys=-1)
    rhs_rows = exchanged(after(rhs, own, two_left, two_right).reshape(Y, BLK, COL))

    lo_far = moved(after(two_left[0], left), xs=1)
    up_far = moved(after(two_right[1], right), xs=-1)

    blocks = (own, left, right, far)
    parts = (near, down, up, below_far, above_far)
    corr_a, sent_a = first_level(FIRST_GROUPS, at, blocks, parts, rhs_rows)
    late = after(at, sent_a)
    corr_b, sent_b = first_level(LAST_GROUPS, late, blocks, parts, rhs_rows)
    below_a, above_a = moved(sent_a, 2), moved(sent_a, -2)
    below_b, above_b = moved(sent_b, 2), moved(sent_b, -2)
    blocks = (lo_two, up_two, two_left, two_right, lo_far, up_far)
    two, one = second_level(FIRST_GROUPS, at, blocks, below_a, above_a, corr_a, rhs)
    late = after(late, two)
    three, total = second_level(
        LAST_GROUPS, late, blocks, below_b, above_b, corr_b, rhs
    )
    for d, part in ((2, two), (1, one), (3, three)):
        total = total + moved(part, ys=d).astype(jnp.float32)
    return total[None]


def solution(mesh):
    fine = Mesh(mesh.devices.reshape(Z, CORES, Y, X), AXES)
    spec = P(("z", "core"), None, ("y", "x"))
    return jax.shard_map(
        on_device,
        mesh=fine,
        in_specs=(spec,) * 5,
        out_specs=spec,
        check_vma=False,
    )
```

```python
import functools
import itertools

import jax
import jax.numpy as jnp
from jax import lax
from jax.experimental import pallas as pl
from jax.experimental.pallas import tpu as pltpu
from jax.sharding import Mesh, PartitionSpec as P

Z, CORES, Y, X = 16, 2, 4, 4
M = 2048
BLK = M // Y
COL = 128
AXES = ("z", "core", "y", "x")


def home(core, x):
    return (core, x) if core == x // 2 else (1 - core, X - 1 - x)


def sent(value, target):
    places = list(itertools.product(range(Z), range(CORES), range(Y), range(X)))
    number = {place: i for i, place in enumerate(places)}
    pairs = [(number[place], number.get(target(*place))) for place in places]
    return lax.ppermute(value, AXES, [pair for pair in pairs if pair[1] is not None])


def along(value, ys=0, zs=0):
    return sent(value, lambda z, core, y, x: (z + zs, core, (y + ys) % Y, x))


def to_home(value, ys=0):
    return sent(
        value,
        lambda z, core, y, x: (z, home(core, x)[0], (y + ys) % Y, home(core, x)[1]),
    )


def to_next_plane(value, step):
    def target(z, core, y, x):
        plane = z * CORES + core + step
        to_core, to_x = home(plane % CORES, x)
        return (plane // CORES, to_core, y, to_x)

    return sent(value, target)


def over_x(value):
    def partner(z, core, y, x):
        to_core, to_x = home(core, x)
        return (z, to_core, y, to_x ^ 1)

    def swapped(part):
        return sent(part, lambda z, core, y, x: (z, 1 - core, y, x))

    near, far = to_home(value), sent(value, partner)
    return near, far, swapped(far), swapped(near)


def after(value, *before):
    return lax.optimization_barrier((value,) + before)[0]


def rows_in_order(at_ref, ref, row):
    starts = [pl.multiple_of((at_ref[1] ^ e) * COL, COL) for e in range(X)]
    return [ref[row + (pl.ds(start, COL),)] for start in starts]


FIRST_GROUPS, LAST_GROUPS = (2, 1), (3, 0)


def first_kernel(groups, at_ref, *refs):
    blocks, parts = refs[:X], refs[X : X + 2 * len(groups)]
    rhs_ref, corr_ref, sent_ref, acc_ref = refs[X + 2 * len(groups) :]
    step = pl.program_id(0)

    @pl.when(step == 0)
    def _():
        acc_ref[...] = jnp.zeros_like(acc_ref)

    total = acc_ref[...]
    for side in (0, 1):
        left = jnp.concatenate([block[0, side] for block in blocks], axis=1)
        right = [
            jnp.concatenate(rows_in_order(at_ref, part, (0,)), axis=0)
            for part in parts[side :: 2]
        ]
        right = jnp.concatenate(right, axis=1)
        total = total + jnp.dot(left, right, preferred_element_type=jnp.float32)
    acc_ref[...] = total

    @pl.when(step == Y - 1)
    def _():
        for i, d in enumerate(groups):
            piece = acc_ref[:, i * COL : (i + 1) * COL]
            corr_ref[i] = piece
            owner = lax.rem(at_ref[0] + d, Y)
            sent_ref[i] = (rhs_ref[owner] + piece).astype(jnp.bfloat16)


def first_level(groups, at, blocks, parts, rhs):
    count = len(groups)
    block = pl.BlockSpec((1, 2, BLK, COL), lambda k, at: (k, 0, 0, 0))
    whole = pl.BlockSpec((Y, BLK, COL), lambda k, at: (0, 0, 0))
    out = pl.BlockSpec((count, BLK, COL), lambda k, at: (0, 0, 0))

    def part(index):
        return pl.BlockSpec((1, BLK, COL), lambda k, at: (index, k, 0))

    return pl.pallas_call(
        functools.partial(first_kernel, groups),
        name="first_level",
        out_shape=(
            jax.ShapeDtypeStruct((count, BLK, COL), jnp.float32),
            jax.ShapeDtypeStruct((count, BLK, COL), jnp.bfloat16),
        ),
        grid_spec=pltpu.PrefetchScalarGridSpec(
            num_scalar_prefetch=1,
            grid=(Y,),
            in_specs=[block] * X + [part(index) for _, index in parts] + [whole],
            out_specs=(out, out),
            scratch_shapes=[pltpu.VMEM((BLK, count * COL), jnp.float32)],
        ),
        compiler_params=pltpu.CompilerParams(vmem_limit_bytes=32 << 20),
        cost_estimate=pl.CostEstimate(
            flops=4 * BLK * M * count * COL,
            bytes_accessed=8 << 20,
            transcendentals=0,
        ),
    )(at, *blocks, *[array for array, _ in parts], rhs)


def second_kernel(groups, at_ref, *refs):
    blocks = refs[:X]
    below, above, corr_ref, *outs = refs[X:]
    step = pl.program_id(0)
    total = None
    for side, b_ref in ((0, below), (1, above)):
        left = jnp.concatenate([block[side] for block in blocks], axis=1)
        right = [
            jnp.concatenate(rows_in_order(at_ref, b_ref, (i,)), axis=0)
            for i in range(len(groups))
        ]
        right = jnp.concatenate(right, axis=1)
        term = jnp.dot(left, right, preferred_element_type=jnp.float32)
        total = term if total is None else total + term
    here = step == at_ref[0]
    for i in range(len(groups)):
        piece = total[:, i * COL : (i + 1) * COL]
        piece = piece + jnp.where(here, corr_ref[i], 0.0)
        outs[i][...] = piece.astype(outs[i].dtype)


def second_level(groups, at, blocks, below, above, corr):
    count = len(groups)
    rows = pl.BlockSpec((BLK, COL), lambda m, at: (m, 0))
    pair = pl.BlockSpec((2, BLK, COL), lambda m, at: (0, m, 0))
    whole = pl.BlockSpec((count, BLK, COL), lambda m, at: (0, 0, 0))
    return pl.pallas_call(
        functools.partial(second_kernel, groups),
        name="second_level",
        out_shape=(jax.ShapeDtypeStruct((M, COL), jnp.bfloat16),) * count,
        grid_spec=pltpu.PrefetchScalarGridSpec(
            num_scalar_prefetch=1,
            grid=(Y,),
            in_specs=[pair] * X + [whole] * 3,
            out_specs=(rows,) * count,
        ),
        compiler_params=pltpu.CompilerParams(vmem_limit_bytes=32 << 20),
        cost_estimate=pl.CostEstimate(
            flops=4 * BLK * M * count * COL,
            bytes_accessed=6 << 20,
            transcendentals=0,
        ),
    )(at, *blocks, below, above, corr)


def on_device(right_sides, lower_first, upper_first, lower_second, upper_second):
    rhs = right_sides[0]
    x = lax.axis_index("x")
    label = jnp.where(lax.axis_index("core") == x >> 1, x, X - 1 - x)
    at = jnp.stack([lax.axis_index("y"), label]).astype(jnp.int32)

    def exchanged(value):
        return lax.all_to_all(value, "y", 0, 0, tiled=True)

    firsts = [v[0].reshape(Y, BLK, COL) for v in (lower_first, upper_first)]
    firsts = jnp.stack(firsts, axis=1)
    sent_one = after(rhs, firsts).astype(jnp.bfloat16)
    own = exchanged(firsts)
    near = jnp.stack([to_next_plane(sent_one, 1), to_next_plane(sent_one, -1)])

    seconds = after(jnp.stack([lower_second[0], upper_second[0]]), sent_one)
    seconds = over_x(seconds)
    firsts = over_x(own)

    down, up = along(near, ys=1), along(near, ys=-1)
    below_far, above_far = along(down[0], ys=1), along(up[1], ys=-1)
    rhs_rows = to_home(exchanged(after(rhs, own).reshape(Y, BLK, COL)))

    parts = ((below_far[None], 0), (above_far[None], 0), (up, 0), (up, 1))
    corr_a, sent_a = first_level(FIRST_GROUPS, at, firsts, parts, rhs_rows)
    late = after(at, sent_a)
    parts = ((down, 0), (down, 1), (near, 0), (near, 1))
    corr_b, sent_b = first_level(LAST_GROUPS, late, firsts, parts, rhs_rows)

    below_a, above_a = along(sent_a, zs=1), along(sent_a, zs=-1)
    below_b, above_b = along(sent_b, zs=1), along(sent_b, zs=-1)
    outs = second_level(FIRST_GROUPS, at, seconds, below_a, above_a, corr_a)
    late = after(late, outs[0])
    outs += second_level(LAST_GROUPS, late, seconds, below_b, above_b, corr_b)
    total = rhs
    for d, part in zip(FIRST_GROUPS + LAST_GROUPS, outs):
        total = total + to_home(part, ys=d).astype(jnp.float32)
    return total[None]


def solution(mesh):
    fine = Mesh(mesh.devices.reshape(Z, CORES, Y, X), AXES)
    spec = P(("z", "core"), None, ("y", "x"))
    return jax.shard_map(
        on_device,
        mesh=fine,
        in_specs=(spec,) * 5,
        out_specs=spec,
        check_vma=False,
    )
```

```python
import functools
import itertools

import jax
import jax.numpy as jnp
from jax import lax
from jax.experimental import pallas as pl
from jax.experimental.pallas import tpu as pltpu
from jax.sharding import Mesh, PartitionSpec as P

Z, CORES, Y, X = 16, 2, 4, 4
M = 2048
BLK = M // Y
COL = 128
AXES = ("z", "core", "y", "x")


def home(core, x):
    return (core, x) if core == x // 2 else (1 - core, X - 1 - x)


def sent(value, target):
    places = list(itertools.product(range(Z), range(CORES), range(Y), range(X)))
    number = {place: i for i, place in enumerate(places)}
    pairs = [(number[place], number.get(target(*place))) for place in places]
    return lax.ppermute(value, AXES, [pair for pair in pairs if pair[1] is not None])


def along(value, ys=0, zs=0):
    return sent(value, lambda z, core, y, x: (z + zs, core, (y + ys) % Y, x))


def to_home(value, ys=0, itself=True):
    def target(z, core, y, x):
        to_core, to_x = home(core, x)
        if to_core == core and not itself:
            return None
        return (z, to_core, (y + ys) % Y, to_x)

    return sent(value, target)


def to_next_plane(value, step):
    def target(z, core, y, x):
        plane = z * CORES + core + step
        to_core, to_x = home(plane % CORES, x)
        return (plane // CORES, to_core, y, to_x)

    return sent(value, target)


def over_x(value):
    def at_home(core, x):
        return core == x // 2

    def near(z, core, y, x):
        return (z, core, y, x ^ 1) if at_home(core, x) else (z, 1 - core, y, x ^ 3)

    def far(z, core, y, x):
        return None if at_home(core, x) else (z, 1 - core, y, x ^ 2)

    def swapped(part, kept=None):
        def target(z, core, y, x):
            if kept is None or at_home(core, x) == kept:
                return (z, 1 - core, y, x)
            return None

        return sent(part, target)

    first, second = sent(value, near), sent(value, far)
    return value, second, first, swapped(value, True), swapped(second, False), swapped(first)


def in_order(at_ref, pieces):
    own, far, near, core_own, core_far, core_near = pieces
    kept = at_ref[2] == 1
    return [
        jnp.where(kept, own, far),
        near,
        jnp.where(kept, core_far, core_own),
        core_near,
    ]


def after(value, *before):
    return lax.optimization_barrier((value,) + before)[0]


def rows_in_order(at_ref, ref, row):
    starts = [pl.multiple_of((at_ref[1] ^ e) * COL, COL) for e in range(X)]
    return [ref[row + (pl.ds(start, COL),)] for start in starts]


FIRST_GROUPS, LAST_GROUPS = (2, 1), (3, 0)
BLOCKS = 6


def first_kernel(groups, at_ref, *refs):
    blocks, parts = refs[:BLOCKS], refs[BLOCKS : BLOCKS + 2 * len(groups)]
    rhs_ref, rhs_home_ref, corr_ref, sent_ref, acc_ref = refs[BLOCKS + 2 * len(groups) :]
    step = pl.program_id(0)

    @pl.when(step == 0)
    def _():
        acc_ref[...] = jnp.zeros_like(acc_ref)

    total = acc_ref[...]
    for side in (0, 1):
        left = in_order(at_ref, [block[0, side] for block in blocks])
        left = jnp.concatenate(left, axis=1)
        right = [
            jnp.concatenate(rows_in_order(at_ref, part, (0,)), axis=0)
            for part in parts[side :: 2]
        ]
        right = jnp.concatenate(right, axis=1)
        total = total + jnp.dot(left, right, preferred_element_type=jnp.float32)
    acc_ref[...] = total

    @pl.when(step == Y - 1)
    def _():
        for i, d in enumerate(groups):
            piece = acc_ref[:, i * COL : (i + 1) * COL]
            corr_ref[i] = piece
            owner = lax.rem(at_ref[0] + d, Y)
            rhs = jnp.where(at_ref[2] == 1, rhs_ref[owner], rhs_home_ref[owner])
            sent_ref[i] = (rhs + piece).astype(jnp.bfloat16)


def first_level(groups, at, blocks, parts, rhs):
    count = len(groups)
    block = pl.BlockSpec((1, 2, BLK, COL), lambda k, at: (k, 0, 0, 0))
    whole = pl.BlockSpec((Y, BLK, COL), lambda k, at: (0, 0, 0))
    out = pl.BlockSpec((count, BLK, COL), lambda k, at: (0, 0, 0))

    def part(index):
        return pl.BlockSpec((1, BLK, COL), lambda k, at: (index, k, 0))

    return pl.pallas_call(
        functools.partial(first_kernel, groups),
        name="first_level",
        out_shape=(
            jax.ShapeDtypeStruct((count, BLK, COL), jnp.float32),
            jax.ShapeDtypeStruct((count, BLK, COL), jnp.bfloat16),
        ),
        grid_spec=pltpu.PrefetchScalarGridSpec(
            num_scalar_prefetch=1,
            grid=(Y,),
            in_specs=[block] * BLOCKS
            + [part(index) for _, index in parts]
            + [whole, whole],
            out_specs=(out, out),
            scratch_shapes=[pltpu.VMEM((BLK, count * COL), jnp.float32)],
        ),
        compiler_params=pltpu.CompilerParams(vmem_limit_bytes=32 << 20),
        cost_estimate=pl.CostEstimate(
            flops=4 * BLK * M * count * COL,
            bytes_accessed=8 << 20,
            transcendentals=0,
        ),
    )(at, *blocks, *[array for array, _ in parts], *rhs)


def second_kernel(groups, at_ref, *refs):
    blocks = refs[:BLOCKS]
    below, above, corr_ref, *outs = refs[BLOCKS:]
    step = pl.program_id(0)
    total = None
    for side, b_ref in ((0, below), (1, above)):
        left = in_order(at_ref, [block[side] for block in blocks])
        left = jnp.concatenate(left, axis=1)
        right = [
            jnp.concatenate(rows_in_order(at_ref, b_ref, (i,)), axis=0)
            for i in range(len(groups))
        ]
        right = jnp.concatenate(right, axis=1)
        term = jnp.dot(left, right, preferred_element_type=jnp.float32)
        total = term if total is None else total + term
    here = step == at_ref[0]
    for i in range(len(groups)):
        piece = total[:, i * COL : (i + 1) * COL]
        piece = piece + jnp.where(here, corr_ref[i], 0.0)
        outs[i][...] = piece.astype(outs[i].dtype)


def second_level(groups, at, blocks, below, above, corr):
    count = len(groups)
    rows = pl.BlockSpec((BLK, COL), lambda m, at: (m, 0))
    pair = pl.BlockSpec((2, BLK, COL), lambda m, at: (0, m, 0))
    whole = pl.BlockSpec((count, BLK, COL), lambda m, at: (0, 0, 0))
    return pl.pallas_call(
        functools.partial(second_kernel, groups),
        name="second_level",
        out_shape=(jax.ShapeDtypeStruct((M, COL), jnp.bfloat16),) * count,
        grid_spec=pltpu.PrefetchScalarGridSpec(
            num_scalar_prefetch=1,
            grid=(Y,),
            in_specs=[pair] * BLOCKS + [whole] * 3,
            out_specs=(rows,) * count,
        ),
        compiler_params=pltpu.CompilerParams(vmem_limit_bytes=32 << 20),
        cost_estimate=pl.CostEstimate(
            flops=4 * BLK * M * count * COL,
            bytes_accessed=6 << 20,
            transcendentals=0,
        ),
    )(at, *blocks, below, above, corr)


def on_device(right_sides, lower_first, upper_first, lower_second, upper_second):
    rhs = right_sides[0]
    x = lax.axis_index("x")
    kept = (lax.axis_index("core") == x >> 1).astype(jnp.int32)
    label = x ^ (2 - 2 * kept)
    at = jnp.stack([lax.axis_index("y"), label, kept]).astype(jnp.int32)

    def exchanged(value):
        return lax.all_to_all(value, "y", 0, 0, tiled=True)

    firsts = [v[0].reshape(Y, BLK, COL) for v in (lower_first, upper_first)]
    firsts = jnp.stack(firsts, axis=1)
    sent_one = after(rhs, firsts).astype(jnp.bfloat16)
    own = exchanged(firsts)
    near = [to_next_plane(sent_one, 1), to_next_plane(sent_one, -1)]
    near = after(jnp.stack(near), own)

    seconds = after(jnp.stack([lower_second[0], upper_second[0]]), sent_one)
    seconds = over_x(seconds)
    firsts = over_x(own)

    down, up = along(near, ys=1), along(near, ys=-1)
    below_far, above_far = along(down[0], ys=1), along(up[1], ys=-1)
    rhs_rows = exchanged(after(rhs, own).reshape(Y, BLK, COL))
    rhs_rows = (rhs_rows, to_home(rhs_rows, itself=False))

    parts = ((below_far[None], 0), (above_far[None], 0), (up, 0), (up, 1))
    corr_a, sent_a = first_level(FIRST_GROUPS, at, firsts, parts, rhs_rows)
    late = after(at, sent_a)
    parts = ((down, 0), (down, 1), (near, 0), (near, 1))
    corr_b, sent_b = first_level(LAST_GROUPS, late, firsts, parts, rhs_rows)

    below_a, above_a = along(sent_a, zs=1), along(sent_a, zs=-1)
    below_b, above_b = along(sent_b, zs=1), along(sent_b, zs=-1)
    outs = second_level(FIRST_GROUPS, at, seconds, below_a, above_a, corr_a)
    late = after(late, outs[0])
    outs += second_level(LAST_GROUPS, late, seconds, below_b, above_b, corr_b)
    total = rhs
    for d, part in zip(FIRST_GROUPS + LAST_GROUPS, outs):
        total = total + to_home(part, ys=d).astype(jnp.float32)
    return total[None]


def solution(mesh):
    fine = Mesh(mesh.devices.reshape(Z, CORES, Y, X), AXES)
    spec = P(("z", "core"), None, ("y", "x"))
    return jax.shard_map(
        on_device,
        mesh=fine,
        in_specs=(spec,) * 5,
        out_specs=spec,
        check_vma=False,
    )
```

```python
import functools

import jax
import jax.numpy as jnp
from jax import lax
from jax.experimental import pallas as pl
from jax.experimental.pallas import tpu as pltpu
from jax.sharding import Mesh, PartitionSpec as P

Z, CORES, Y, X = 16, 2, 4, 4
PLANES = Z * CORES
M = 2048
BLK = M // Y
COL = 128
AXES = ("z", "core", "y", "x")


def device_index(plane, y, x):
    return (plane * Y + y) * X + x


def moved(value, planes=0, ys=0, xs=0):
    pairs = []
    for plane in range(PLANES):
        if not 0 <= plane + planes < PLANES:
            continue
        for y in range(Y):
            for x in range(X):
                target = device_index(plane + planes, (y + ys) % Y, (x + xs) % X)
                pairs.append((device_index(plane, y, x), target))
    return lax.ppermute(value, AXES, pairs)


def after(value, *before):
    return lax.optimization_barrier((value,) + before)[0]


def rows_in_order(at_ref, ref, index, start):
    starts = [start + lax.rem(at_ref[1] + e, X) * COL for e in range(X)]
    return [ref[index + (pl.ds(pl.multiple_of(at, COL), COL),)] for at in starts]


FIRST_GROUPS, LAST_GROUPS = (2, 1), (3, 0)


def first_kernel(groups, at_ref, *refs):
    blocks, parts = refs[:X], refs[X : X + 2 * len(groups)]
    rhs_ref, corr_ref, sent_ref = refs[X + 2 * len(groups) :]
    indices = [index for _, index in part_places(groups)]

    total = jnp.zeros((BLK, len(groups) * COL), jnp.float32)
    for k in range(Y):
        for side in (0, 1):
            left = jnp.concatenate([block[k, side] for block in blocks], axis=1)
            right = []
            for part, index in list(zip(parts, indices))[side::2]:
                rows = rows_in_order(at_ref, part, index, k * BLK)
                right.append(jnp.concatenate(rows, axis=0))
            right = jnp.concatenate(right, axis=1)
            total = total + jnp.dot(left, right, preferred_element_type=jnp.float32)

    for i, d in enumerate(groups):
        piece = total[:, i * COL : (i + 1) * COL]
        corr_ref[i] = piece
        owner = lax.rem(at_ref[0] + d, Y)
        sent_ref[i] = (rhs_ref[owner] + piece).astype(jnp.bfloat16)


def part_places(groups):
    places = {
        0: (("near", (0,)), ("near", (1,))),
        1: (("up", (0,)), ("up", (1,))),
        2: (("below_far", ()), ("above_far", ())),
        3: (("down", (0,)), ("down", (1,))),
    }
    return [place for d in groups for place in places[d]]


IN_SMEM = pl.BlockSpec(memory_space=pltpu.SMEM)
IN_VMEM = pl.BlockSpec(memory_space=pltpu.VMEM)


def first_level(groups, at, blocks, parts, rhs):
    count = len(groups)
    parts = [parts[name] for name, _ in part_places(groups)]
    return pl.pallas_call(
        functools.partial(first_kernel, groups),
        name="first_level",
        out_shape=(
            jax.ShapeDtypeStruct((count, BLK, COL), jnp.float32),
            jax.ShapeDtypeStruct((count, BLK, COL), jnp.bfloat16),
        ),
        in_specs=[IN_SMEM] + [IN_VMEM] * (X + len(parts) + 1),
        out_specs=(IN_VMEM, IN_VMEM),
        compiler_params=pltpu.CompilerParams(vmem_limit_bytes=24 << 20),
        cost_estimate=pl.CostEstimate(
            flops=4 * BLK * M * count * COL,
            bytes_accessed=8 << 20,
            transcendentals=0,
        ),
    )(at, *blocks, *parts, rhs)


def second_kernel(groups, at_ref, *refs):
    lower, upper = refs[:X], refs[X : 2 * X]
    below, above, corr_ref, *outs = refs[2 * X :]

    for m in range(Y):
        rows = pl.ds(m * BLK, BLK)
        total = None
        for blocks, b_ref in ((lower, below), (upper, above)):
            left = jnp.concatenate([block[rows, :] for block in blocks], axis=1)
            right = [
                jnp.concatenate(rows_in_order(at_ref, b_ref, (i,), 0), axis=0)
                for i in range(len(groups))
            ]
            right = jnp.concatenate(right, axis=1)
            term = jnp.dot(left, right, preferred_element_type=jnp.float32)
            total = term if total is None else total + term
        here = m == at_ref[0]
        for i in range(len(groups)):
            piece = total[:, i * COL : (i + 1) * COL]
            piece = piece + jnp.where(here, corr_ref[i], 0.0)
            outs[i][rows, :] = piece.astype(outs[i].dtype)


def second_level(groups, at, blocks, below, above, corr):
    return pl.pallas_call(
        functools.partial(second_kernel, groups),
        name="second_level",
        out_shape=tuple(
            jax.ShapeDtypeStruct((M, COL), jnp.bfloat16 if d else jnp.float32)
            for d in groups
        ),
        in_specs=[IN_SMEM] + [IN_VMEM] * (2 * X + 3),
        out_specs=(IN_VMEM,) * len(groups),
        compiler_params=pltpu.CompilerParams(vmem_limit_bytes=24 << 20),
        cost_estimate=pl.CostEstimate(
            flops=4 * BLK * M * len(groups) * COL,
            bytes_accessed=6 << 20,
            transcendentals=0,
        ),
    )(at, *blocks, below, above, corr)


def on_device(right_sides, lower_first, upper_first, lower_second, upper_second):
    rhs = right_sides[0]
    at = jnp.stack([lax.axis_index("y"), lax.axis_index("x")]).astype(jnp.int32)

    def exchanged(value):
        return lax.all_to_all(value, "y", 0, 0, tiled=True)

    firsts = [v[0].reshape(Y, BLK, COL) for v in (lower_first, upper_first)]
    firsts = jnp.stack(firsts, axis=1)
    sent_one = after(rhs, firsts).astype(jnp.bfloat16)
    own = exchanged(firsts)
    near = jnp.stack([moved(sent_one, 1), moved(sent_one, -1)])
    near = after(near, own)

    lo, up = after(lower_second[0], sent_one), upper_second[0]
    lo_left, lo_right = moved(lo, xs=1), moved(lo, xs=-1)

    sent_own = after(own, lo_left, lo_right)
    left, right = moved(sent_own, xs=1), moved(sent_own, xs=-1)
    far = moved(sent_own, xs=2)
    from_down, from_up = moved(near, ys=1), moved(near, ys=-1)
    below_far = moved(from_down[0], ys=1)
    above_far = moved(from_up[1], ys=-1)
    rhs_rows = exchanged(after(rhs, own).reshape(Y, BLK, COL))

    up = after(up, from_down, from_up)
    up_left, up_right = moved(up, xs=1), moved(up, xs=-1)
    lo_far = moved(after(lo_left, from_down, from_up), xs=1)
    up_far = moved(up_right, xs=-1)

    blocks = (own, right, far, left)
    parts = dict(near=near, up=from_up, down=from_down)
    parts.update(below_far=below_far, above_far=above_far)
    corr_a, sent_a = first_level(FIRST_GROUPS, at, blocks, parts, rhs_rows)
    late = after(at, sent_a)
    corr_b, sent_b = first_level(LAST_GROUPS, late, blocks, parts, rhs_rows)
    below_a, above_a = moved(sent_a, 2), moved(sent_a, -2)
    below_b, above_b = moved(sent_b, 2), moved(sent_b, -2)
    blocks = (lo, lo_right, lo_far, lo_left, up, up_right, up_far, up_left)
    two, one = second_level(FIRST_GROUPS, at, blocks, below_a, above_a, corr_a)
    late = after(late, two)
    three, total = second_level(LAST_GROUPS, late, blocks, below_b, above_b, corr_b)
    total = total + rhs
    for d, part in ((2, two), (1, one), (3, three)):
        total = total + moved(part, ys=d).astype(jnp.float32)
    return total[None]


def solution(mesh):
    fine = Mesh(mesh.devices.reshape(Z, CORES, Y, X), AXES)
    spec = P(("z", "core"), None, ("y", "x"))
    return jax.shard_map(
        on_device,
        mesh=fine,
        in_specs=(spec,) * 5,
        out_specs=spec,
        check_vma=False,
    )
```

```python
import functools

import jax
import jax.numpy as jnp
from jax import lax
from jax.experimental import pallas as pl
from jax.experimental.pallas import tpu as pltpu
from jax.sharding import Mesh, PartitionSpec as P

Z, CORES, Y, X = 16, 2, 4, 4
PLANES = Z * CORES
M = 2048
BLK = M // Y
COL = 128
AXES = ("z", "core", "y", "x")


def device_index(plane, y, x):
    return (plane * Y + y) * X + x


def moved(value, planes=0, ys=0, xs=0):
    pairs = []
    for plane in range(PLANES):
        if not 0 <= plane + planes < PLANES:
            continue
        for y in range(Y):
            for x in range(X):
                target = device_index(plane + planes, (y + ys) % Y, (x + xs) % X)
                pairs.append((device_index(plane, y, x), target))
    return lax.ppermute(value, AXES, pairs)


def after(value, *before):
    return lax.optimization_barrier((value,) + before)[0]


def rows_in_order(at_ref, ref, index, start):
    starts = [start + lax.rem(at_ref[1] + e, X) * COL for e in range(X)]
    return [ref[index + (pl.ds(pl.multiple_of(at, COL), COL),)] for at in starts]


FIRST_GROUPS, LAST_GROUPS = (2, 1), (3, 0)


def first_kernel(groups, at_ref, *refs):
    blocks, parts = refs[:X], refs[X : X + 2 * len(groups)]
    rhs_ref, corr_ref, sent_ref = refs[X + 2 * len(groups) :]
    indices = [index for _, index in part_places(groups)]

    total = jnp.zeros((BLK, len(groups) * COL), jnp.float32)
    for k in range(Y):
        for side in (0, 1):
            left = jnp.concatenate([block[k, side] for block in blocks], axis=1)
            right = []
            for part, index in list(zip(parts, indices))[side::2]:
                rows = rows_in_order(at_ref, part, index, k * BLK)
                right.append(jnp.concatenate(rows, axis=0))
            right = jnp.concatenate(right, axis=1)
            total = total + jnp.dot(left, right, preferred_element_type=jnp.float32)

    for i, d in enumerate(groups):
        piece = total[:, i * COL : (i + 1) * COL]
        corr_ref[i] = piece
        owner = lax.rem(at_ref[0] + d, Y)
        sent_ref[i] = (rhs_ref[owner] + piece).astype(jnp.bfloat16)


def part_places(groups):
    places = {
        0: (("near", (0,)), ("near", (1,))),
        1: (("up", (0,)), ("up", (1,))),
        2: (("far", (0,)), ("far", (1,))),
        3: (("down", (0,)), ("down", (1,))),
    }
    return [place for d in groups for place in places[d]]


IN_SMEM = pl.BlockSpec(memory_space=pltpu.SMEM)
IN_VMEM = pl.BlockSpec(memory_space=pltpu.VMEM)


def first_level(groups, at, blocks, parts, rhs):
    count = len(groups)
    parts = [parts[name] for name, _ in part_places(groups)]
    return pl.pallas_call(
        functools.partial(first_kernel, groups),
        name="first_level",
        out_shape=(
            jax.ShapeDtypeStruct((count, BLK, COL), jnp.float32),
            jax.ShapeDtypeStruct((count, BLK, COL), jnp.bfloat16),
        ),
        in_specs=[IN_SMEM] + [IN_VMEM] * (X + len(parts) + 1),
        out_specs=(IN_VMEM, IN_VMEM),
        compiler_params=pltpu.CompilerParams(vmem_limit_bytes=24 << 20),
        cost_estimate=pl.CostEstimate(
            flops=4 * BLK * M * count * COL,
            bytes_accessed=8 << 20,
            transcendentals=0,
        ),
    )(at, *blocks, *parts, rhs)


def second_kernel(groups, at_ref, *refs):
    blocks = refs[:X]
    below, above, corr_ref, *outs = refs[X:]

    for m in range(Y):
        rows = pl.ds(m * BLK, BLK)
        total = None
        for side, b_ref in ((0, below), (1, above)):
            left = jnp.concatenate([block[side, rows, :] for block in blocks], axis=1)
            right = [
                jnp.concatenate(rows_in_order(at_ref, b_ref, (i,), 0), axis=0)
                for i in range(len(groups))
            ]
            right = jnp.concatenate(right, axis=1)
            term = jnp.dot(left, right, preferred_element_type=jnp.float32)
            total = term if total is None else total + term
        here = m == at_ref[0]
        for i in range(len(groups)):
            piece = total[:, i * COL : (i + 1) * COL]
            piece = piece + jnp.where(here, corr_ref[i], 0.0)
            outs[i][rows, :] = piece.astype(outs[i].dtype)


def second_level(groups, at, blocks, below, above, corr):
    return pl.pallas_call(
        functools.partial(second_kernel, groups),
        name="second_level",
        out_shape=tuple(
            jax.ShapeDtypeStruct((M, COL), jnp.bfloat16 if d else jnp.float32)
            for d in groups
        ),
        in_specs=[IN_SMEM] + [IN_VMEM] * (X + 3),
        out_specs=(IN_VMEM,) * len(groups),
        compiler_params=pltpu.CompilerParams(vmem_limit_bytes=24 << 20),
        cost_estimate=pl.CostEstimate(
            flops=4 * BLK * M * len(groups) * COL,
            bytes_accessed=6 << 20,
            transcendentals=0,
        ),
    )(at, *blocks, below, above, corr)


def on_device(right_sides, lower_first, upper_first, lower_second, upper_second):
    rhs = right_sides[0]
    at = jnp.stack([lax.axis_index("y"), lax.axis_index("x")]).astype(jnp.int32)

    def exchanged(value):
        return lax.all_to_all(value, "y", 0, 0, tiled=True)

    firsts = [v[0].reshape(Y, BLK, COL) for v in (lower_first, upper_first)]
    firsts = jnp.stack(firsts, axis=1)
    sent_one = after(rhs, firsts).astype(jnp.bfloat16)
    own = exchanged(firsts)
    near = jnp.stack([moved(sent_one, 1), moved(sent_one, -1)])

    seconds = jnp.stack([lower_second[0], upper_second[0]])
    seconds = after(seconds, sent_one)
    two_left, two_right = moved(seconds, xs=1), moved(seconds, xs=-1)

    ready = after(own, near)
    left, right, far = moved(ready, xs=1), moved(ready, xs=-1), moved(ready, xs=2)
    parts = dict(near=near, down=moved(near, ys=1), up=moved(near, ys=-1))
    parts["far"] = moved(after(near, own), ys=2)
    rhs_rows = exchanged(after(rhs, own, two_left, two_right).reshape(Y, BLK, COL))
    two_far = moved(after(seconds, left, right), xs=2)

    blocks = (own, right, far, left)
    corr_a, sent_a = first_level(FIRST_GROUPS, at, blocks, parts, rhs_rows)
    late = after(at, sent_a)
    corr_b, sent_b = first_level(LAST_GROUPS, late, blocks, parts, rhs_rows)
    below_a, above_a = moved(sent_a, 2), moved(sent_a, -2)
    below_b, above_b = moved(sent_b, 2), moved(sent_b, -2)
    blocks = (seconds, two_right, two_far, two_left)
    two, one = second_level(FIRST_GROUPS, at, blocks, below_a, above_a, corr_a)
    late = after(late, two)
    three, total = second_level(LAST_GROUPS, late, blocks, below_b, above_b, corr_b)
    total = total + rhs
    for d, part in ((2, two), (1, one), (3, three)):
        total = total + moved(part, ys=d).astype(jnp.float32)
    return total[None]


def solution(mesh):
    fine = Mesh(mesh.devices.reshape(Z, CORES, Y, X), AXES)
    spec = P(("z", "core"), None, ("y", "x"))
    return jax.shard_map(
        on_device,
        mesh=fine,
        in_specs=(spec,) * 5,
        out_specs=spec,
        check_vma=False,
    )
```

```python
import functools

import jax
import jax.numpy as jnp
from jax import lax
from jax.experimental import pallas as pl
from jax.experimental.pallas import tpu as pltpu
from jax.sharding import Mesh, PartitionSpec as P

Z, CORES, Y, X = 16, 2, 4, 4
PLANES = Z * CORES
M = 2048
BLK = M // Y
COL = 128
AXES = ("z", "core", "y", "x")


def device_index(plane, y, x):
    return (plane * Y + y) * X + x


def moved(value, planes=0, ys=0, xs=0):
    pairs = []
    for plane in range(PLANES):
        if not 0 <= plane + planes < PLANES:
            continue
        for y in range(Y):
            for x in range(X):
                target = device_index(plane + planes, (y + ys) % Y, (x + xs) % X)
                pairs.append((device_index(plane, y, x), target))
    return lax.ppermute(value, AXES, pairs)


def after(value, *before):
    return lax.optimization_barrier((value,) + before)[0]


def rows_in_order(at_ref, ref, index, start):
    starts = [start + lax.rem(at_ref[1] + e, X) * COL for e in range(X)]
    return [ref[index + (pl.ds(pl.multiple_of(at, COL), COL),)] for at in starts]


FIRST_GROUPS, LAST_GROUPS = (2, 1), (3, 0)


def first_kernel(groups, at_ref, *refs):
    blocks, parts = refs[:X], refs[X : X + 2 * len(groups)]
    rhs_ref, corr_ref, sent_ref = refs[X + 2 * len(groups) :]
    indices = [index for _, index in part_places(groups)]

    total = jnp.zeros((BLK, len(groups) * COL), jnp.float32)
    for k in range(Y):
        for side in (0, 1):
            left = jnp.concatenate([block[k, side] for block in blocks], axis=1)
            right = []
            for part, index in list(zip(parts, indices))[side::2]:
                rows = rows_in_order(at_ref, part, index, k * BLK)
                right.append(jnp.concatenate(rows, axis=0))
            right = jnp.concatenate(right, axis=1)
            total = total + jnp.dot(left, right, preferred_element_type=jnp.float32)

    for i, d in enumerate(groups):
        piece = total[:, i * COL : (i + 1) * COL]
        corr_ref[i] = piece
        owner = lax.rem(at_ref[0] + d, Y)
        sent_ref[i] = (rhs_ref[owner] + piece).astype(jnp.bfloat16)


def part_places(groups):
    places = {
        0: (("near", (0,)), ("near", (1,))),
        1: (("up", (0,)), ("up", (1,))),
        2: (("below_far", ()), ("above_far", ())),
        3: (("down", (0,)), ("down", (1,))),
    }
    return [place for d in groups for place in places[d]]


IN_SMEM = pl.BlockSpec(memory_space=pltpu.SMEM)
IN_VMEM = pl.BlockSpec(memory_space=pltpu.VMEM)


def first_level(groups, at, blocks, parts, rhs):
    count = len(groups)
    parts = [parts[name] for name, _ in part_places(groups)]
    return pl.pallas_call(
        functools.partial(first_kernel, groups),
        name="first_level",
        out_shape=(
            jax.ShapeDtypeStruct((count, BLK, COL), jnp.float32),
            jax.ShapeDtypeStruct((count, BLK, COL), jnp.bfloat16),
        ),
        in_specs=[IN_SMEM] + [IN_VMEM] * (X + len(parts) + 1),
        out_specs=(IN_VMEM, IN_VMEM),
        compiler_params=pltpu.CompilerParams(vmem_limit_bytes=24 << 20),
        cost_estimate=pl.CostEstimate(
            flops=4 * BLK * M * count * COL,
            bytes_accessed=8 << 20,
            transcendentals=0,
        ),
    )(at, *blocks, *parts, rhs)


def second_kernel(groups, at_ref, *refs):
    lo, up, left, right, lo_far, up_far = refs[:6]
    lower = (lo, right.at[0], lo_far, left.at[0])
    upper = (up, right.at[1], up_far, left.at[1])
    below, above, corr_ref, *outs = refs[6:]

    for m in range(Y):
        rows = pl.ds(m * BLK, BLK)
        total = None
        for blocks, b_ref in ((lower, below), (upper, above)):
            blocks = [block[rows, :] for block in blocks]
            left = jnp.concatenate(blocks, axis=1)
            right = [
                jnp.concatenate(rows_in_order(at_ref, b_ref, (i,), 0), axis=0)
                for i in range(len(groups))
            ]
            right = jnp.concatenate(right, axis=1)
            term = jnp.dot(left, right, preferred_element_type=jnp.float32)
            total = term if total is None else total + term
        here = m == at_ref[0]
        for i in range(len(groups)):
            piece = total[:, i * COL : (i + 1) * COL]
            piece = piece + jnp.where(here, corr_ref[i], 0.0)
            outs[i][rows, :] = piece.astype(outs[i].dtype)


def second_level(groups, at, blocks, below, above, corr):
    return pl.pallas_call(
        functools.partial(second_kernel, groups),
        name="second_level",
        out_shape=tuple(
            jax.ShapeDtypeStruct((M, COL), jnp.bfloat16 if d else jnp.float32)
            for d in groups
        ),
        in_specs=[IN_SMEM] + [IN_VMEM] * 9,
        out_specs=(IN_VMEM,) * len(groups),
        compiler_params=pltpu.CompilerParams(vmem_limit_bytes=24 << 20),
        cost_estimate=pl.CostEstimate(
            flops=4 * BLK * M * len(groups) * COL,
            bytes_accessed=6 << 20,
            transcendentals=0,
        ),
    )(at, *blocks, below, above, corr)


def on_device(right_sides, lower_first, upper_first, lower_second, upper_second):
    rhs = right_sides[0]
    at = jnp.stack([lax.axis_index("y"), lax.axis_index("x")]).astype(jnp.int32)

    def exchanged(value):
        return lax.all_to_all(value, "y", 0, 0, tiled=True)

    firsts = [v[0].reshape(Y, BLK, COL) for v in (lower_first, upper_first)]
    firsts = jnp.stack(firsts, axis=1)
    sent_one = after(rhs, firsts).astype(jnp.bfloat16)
    own = exchanged(firsts)
    near = jnp.stack([moved(sent_one, 1), moved(sent_one, -1)])

    lo_two, up_two = lower_second[0], upper_second[0]
    seconds = after(jnp.stack([lo_two, up_two]), sent_one)
    two_left, two_right = moved(seconds, xs=1), moved(seconds, xs=-1)

    left, right, far = moved(own, xs=1), moved(own, xs=-1), moved(own, xs=2)
    down, up = moved(near, ys=1), moved(near, ys=-1)
    below_far, above_far = moved(down[0], ys=1), moved(up[1], ys=-1)
    rhs_rows = exchanged(after(rhs, own, two_left, two_right).reshape(Y, BLK, COL))

    lo_far = moved(after(two_left[0], left), xs=1)
    up_far = moved(after(two_right[1], right), xs=-1)

    blocks = (own, right, far, left)
    parts = dict(near=near, down=down, up=up)
    parts.update(below_far=below_far, above_far=above_far)
    corr_a, sent_a = first_level(FIRST_GROUPS, at, blocks, parts, rhs_rows)
    late = after(at, sent_a)
    corr_b, sent_b = first_level(LAST_GROUPS, late, blocks, parts, rhs_rows)
    below_a, above_a = moved(sent_a, 2), moved(sent_a, -2)
    below_b, above_b = moved(sent_b, 2), moved(sent_b, -2)
    blocks = (lo_two, up_two, two_left, two_right, lo_far, up_far)
    two, one = second_level(FIRST_GROUPS, at, blocks, below_a, above_a, corr_a)
    late = after(late, two)
    three, total = second_level(LAST_GROUPS, late, blocks, below_b, above_b, corr_b)
    total = total + rhs
    for d, part in ((2, two), (1, one), (3, three)):
        total = total + moved(part, ys=d).astype(jnp.float32)
    return total[None]


def solution(mesh):
    fine = Mesh(mesh.devices.reshape(Z, CORES, Y, X), AXES)
    spec = P(("z", "core"), None, ("y", "x"))
    return jax.shard_map(
        on_device,
        mesh=fine,
        in_specs=(spec,) * 5,
        out_specs=spec,
        check_vma=False,
    )
```

```python
import functools

import jax
import jax.numpy as jnp
from jax import lax
from jax.experimental import pallas as pl
from jax.experimental.pallas import tpu as pltpu
from jax.sharding import Mesh, PartitionSpec as P

Z, CORES, Y, X = 16, 2, 4, 4
PLANES = Z * CORES
M = 2048
BLK = M // Y
COL = 128
AXES = ("z", "core", "y", "x")


def device_index(plane, y, x):
    return (plane * Y + y) * X + x


def moved(value, planes=0, ys=0, xs=0):
    pairs = []
    for plane in range(PLANES):
        if not 0 <= plane + planes < PLANES:
            continue
        for y in range(Y):
            for x in range(X):
                target = device_index(plane + planes, (y + ys) % Y, (x + xs) % X)
                pairs.append((device_index(plane, y, x), target))
    return lax.ppermute(value, AXES, pairs)


def after(value, *before):
    return lax.optimization_barrier((value,) + before)[0]


def rows_in_order(at_ref, ref, index, start):
    starts = [start + lax.rem(at_ref[1] + e, X) * COL for e in range(X)]
    return [ref[index + (pl.ds(pl.multiple_of(at, COL), COL),)] for at in starts]


FIRST_GROUPS, LAST_GROUPS = (2, 1), (3, 0)


def first_kernel(groups, at_ref, *refs):
    blocks, parts = refs[:X], refs[X : X + 2 * len(groups)]
    rhs_ref, corr_ref, sent_ref = refs[X + 2 * len(groups) :]
    indices = [index for _, index in part_places(groups)]

    total = jnp.zeros((BLK, len(groups) * COL), jnp.float32)
    for k in range(Y):
        for side in (0, 1):
            left = jnp.concatenate([block[k, side] for block in blocks], axis=1)
            right = []
            for part, index in list(zip(parts, indices))[side::2]:
                rows = rows_in_order(at_ref, part, index, k * BLK)
                right.append(jnp.concatenate(rows, axis=0))
            right = jnp.concatenate(right, axis=1)
            total = total + jnp.dot(left, right, preferred_element_type=jnp.float32)

    for i, d in enumerate(groups):
        piece = total[:, i * COL : (i + 1) * COL]
        corr_ref[i] = piece
        owner = lax.rem(at_ref[0] + d, Y)
        sent_ref[i] = (rhs_ref[owner] + piece).astype(jnp.bfloat16)


def part_places(groups):
    places = {
        0: (("near", (0,)), ("near", (1,))),
        1: (("up", (0,)), ("up", (1,))),
        2: (("below_far", ()), ("above_far", ())),
        3: (("down", (0,)), ("down", (1,))),
    }
    return [place for d in groups for place in places[d]]


IN_SMEM = pl.BlockSpec(memory_space=pltpu.SMEM)
IN_VMEM = pl.BlockSpec(memory_space=pltpu.VMEM)


def first_level(groups, at, blocks, parts, rhs):
    count = len(groups)
    parts = [parts[name] for name, _ in part_places(groups)]
    return pl.pallas_call(
        functools.partial(first_kernel, groups),
        name="first_level",
        out_shape=(
            jax.ShapeDtypeStruct((count, BLK, COL), jnp.float32),
            jax.ShapeDtypeStruct((count, BLK, COL), jnp.bfloat16),
        ),
        in_specs=[IN_SMEM] + [IN_VMEM] * (X + len(parts) + 1),
        out_specs=(IN_VMEM, IN_VMEM),
        compiler_params=pltpu.CompilerParams(vmem_limit_bytes=24 << 20),
        cost_estimate=pl.CostEstimate(
            flops=4 * BLK * M * count * COL,
            bytes_accessed=8 << 20,
            transcendentals=0,
        ),
    )(at, *blocks, *parts, rhs)


def second_kernel(groups, at_ref, *refs):
    lo, up, left, right, lo_far, up_far = refs[:6]
    lower = (lo, right.at[0], lo_far, left.at[0])
    upper = (up, right.at[1], up_far, left.at[1])
    below, above, corr_ref, *outs = refs[6:]

    for m in range(Y):
        rows = pl.ds(m * BLK, BLK)
        total = None
        for blocks, b_ref in ((lower, below), (upper, above)):
            blocks = [block[rows, :] for block in blocks]
            left = jnp.concatenate(blocks, axis=1)
            right = [
                jnp.concatenate(rows_in_order(at_ref, b_ref, (i,), 0), axis=0)
                for i in range(len(groups))
            ]
            right = jnp.concatenate(right, axis=1)
            term = jnp.dot(left, right, preferred_element_type=jnp.float32)
            total = term if total is None else total + term
        here = m == at_ref[0]
        for i in range(len(groups)):
            piece = total[:, i * COL : (i + 1) * COL]
            piece = piece + jnp.where(here, corr_ref[i], 0.0)
            outs[i][rows, :] = piece.astype(outs[i].dtype)


def second_level(groups, at, blocks, below, above, corr):
    return pl.pallas_call(
        functools.partial(second_kernel, groups),
        name="second_level",
        out_shape=tuple(
            jax.ShapeDtypeStruct((M, COL), jnp.bfloat16 if d else jnp.float32)
            for d in groups
        ),
        in_specs=[IN_SMEM] + [IN_VMEM] * 9,
        out_specs=(IN_VMEM,) * len(groups),
        compiler_params=pltpu.CompilerParams(vmem_limit_bytes=24 << 20),
        cost_estimate=pl.CostEstimate(
            flops=4 * BLK * M * len(groups) * COL,
            bytes_accessed=6 << 20,
            transcendentals=0,
        ),
    )(at, *blocks, below, above, corr)


def on_device(right_sides, lower_first, upper_first, lower_second, upper_second):
    rhs = right_sides[0]
    at = jnp.stack([lax.axis_index("y"), lax.axis_index("x")]).astype(jnp.int32)

    def exchanged(value):
        return lax.all_to_all(value, "y", 0, 0, tiled=True)

    firsts = [v[0].reshape(Y, BLK, COL) for v in (lower_first, upper_first)]
    firsts = jnp.stack(firsts, axis=1)
    sent_one = after(rhs, firsts).astype(jnp.bfloat16)
    own = exchanged(firsts)
    near = jnp.stack([moved(sent_one, 1), moved(sent_one, -1)])

    lo_two, up_two = lower_second[0], upper_second[0]
    seconds = after(jnp.stack([lo_two, up_two]), sent_one)
    two_left, two_right = moved(seconds, xs=1), moved(seconds, xs=-1)

    left, right, far = moved(own, xs=1), moved(own, xs=-1), moved(own, xs=2)
    shared = after(near, own)
    down, up = moved(shared, ys=1), moved(shared, ys=-1)
    below_far, above_far = moved(down[0], ys=1), moved(up[1], ys=-1)
    rhs_rows = exchanged(after(rhs, own, two_left, two_right).reshape(Y, BLK, COL))

    lo_far = moved(after(two_left[0], left), xs=1)
    up_far = moved(after(two_right[1], right), xs=-1)

    blocks = (own, right, far, left)
    parts = dict(near=near, down=down, up=up)
    parts.update(below_far=below_far, above_far=above_far)
    corr_a, sent_a = first_level(FIRST_GROUPS, at, blocks, parts, rhs_rows)
    late = after(at, sent_a)
    corr_b, sent_b = first_level(LAST_GROUPS, late, blocks, parts, rhs_rows)
    below_a, above_a = moved(sent_a, 2), moved(sent_a, -2)
    below_b, above_b = moved(sent_b, 2), moved(sent_b, -2)
    blocks = (lo_two, up_two, two_left, two_right, lo_far, up_far)
    two, one = second_level(FIRST_GROUPS, at, blocks, below_a, above_a, corr_a)
    late = after(late, two)
    three, total = second_level(LAST_GROUPS, late, blocks, below_b, above_b, corr_b)
    total = total + rhs
    for d, part in ((2, two), (1, one), (3, three)):
        total = total + moved(part, ys=d).astype(jnp.float32)
    return total[None]


def solution(mesh):
    fine = Mesh(mesh.devices.reshape(Z, CORES, Y, X), AXES)
    spec = P(("z", "core"), None, ("y", "x"))
    return jax.shard_map(
        on_device,
        mesh=fine,
        in_specs=(spec,) * 5,
        out_specs=spec,
        check_vma=False,
    )
```

```python
import functools

import jax
import jax.numpy as jnp
from jax import lax
from jax.experimental import pallas as pl
from jax.experimental.pallas import tpu as pltpu
from jax.sharding import Mesh, PartitionSpec as P

Z, CORES, Y, X = 16, 2, 4, 4
PLANES = Z * CORES
M = 2048
BLK = M // Y
COL = 128
AXES = ("z", "core", "y", "x")


def device_index(plane, y, x):
    return (plane * Y + y) * X + x


def moved(value, planes=0, ys=0, xs=0):
    pairs = []
    for plane in range(PLANES):
        if not 0 <= plane + planes < PLANES:
            continue
        for y in range(Y):
            for x in range(X):
                target = device_index(plane + planes, (y + ys) % Y, (x + xs) % X)
                pairs.append((device_index(plane, y, x), target))
    return lax.ppermute(value, AXES, pairs)


def after(value, *before):
    return lax.optimization_barrier((value,) + before)[0]


def rows_in_order(at_ref, ref, index, start):
    starts = [start + lax.rem(at_ref[1] + e, X) * COL for e in range(X)]
    return [ref[index + (pl.ds(pl.multiple_of(at, COL), COL),)] for at in starts]


FIRST_GROUPS, LAST_GROUPS = (2, 1), (3, 0)


def first_kernel(groups, at_ref, *refs):
    own, right_ref, *far, left_ref = refs[: X + 1]
    refs = refs[X + 1 :]
    parts = refs[: 2 * len(groups)]
    rhs_ref, corr_ref, sent_ref = refs[2 * len(groups) :]
    indices = [index for _, index in part_places(groups)]

    total = jnp.zeros((BLK, len(groups) * COL), jnp.float32)
    for k in range(Y):
        for side in (0, 1):
            half, row = divmod(k, Y // 2)
            left = [own[k, side], right_ref[k, side]]
            left += [far[half][row, side], left_ref[k, side]]
            left = jnp.concatenate(left, axis=1)
            right = []
            for part, index in list(zip(parts, indices))[side::2]:
                rows = rows_in_order(at_ref, part, index, k * BLK)
                right.append(jnp.concatenate(rows, axis=0))
            right = jnp.concatenate(right, axis=1)
            total = total + jnp.dot(left, right, preferred_element_type=jnp.float32)

    for i, d in enumerate(groups):
        piece = total[:, i * COL : (i + 1) * COL]
        corr_ref[i] = piece
        owner = lax.rem(at_ref[0] + d, Y)
        sent_ref[i] = (rhs_ref[owner] + piece).astype(jnp.bfloat16)


def part_places(groups):
    places = {
        0: (("near", (0,)), ("near", (1,))),
        1: (("up", (0,)), ("up", (1,))),
        2: (("far", (0,)), ("far", (1,))),
        3: (("down", (0,)), ("down", (1,))),
    }
    return [place for d in groups for place in places[d]]


IN_SMEM = pl.BlockSpec(memory_space=pltpu.SMEM)
IN_VMEM = pl.BlockSpec(memory_space=pltpu.VMEM)


def first_level(groups, at, blocks, parts, rhs):
    count = len(groups)
    parts = [parts[name] for name, _ in part_places(groups)]
    return pl.pallas_call(
        functools.partial(first_kernel, groups),
        name="first_level",
        out_shape=(
            jax.ShapeDtypeStruct((count, BLK, COL), jnp.float32),
            jax.ShapeDtypeStruct((count, BLK, COL), jnp.bfloat16),
        ),
        in_specs=[IN_SMEM] + [IN_VMEM] * (X + len(parts) + 2),
        out_specs=(IN_VMEM, IN_VMEM),
        compiler_params=pltpu.CompilerParams(vmem_limit_bytes=24 << 20),
        cost_estimate=pl.CostEstimate(
            flops=4 * BLK * M * count * COL,
            bytes_accessed=8 << 20,
            transcendentals=0,
        ),
    )(at, *blocks, *parts, rhs)


def second_kernel(groups, at_ref, *refs):
    lo, up, left, right, lo_far, up_far = refs[:6]
    lower = (lo, right.at[0], lo_far, left.at[0])
    upper = (up, right.at[1], up_far, left.at[1])
    below, above, corr_ref, *outs = refs[6:]

    for m in range(Y):
        rows = pl.ds(m * BLK, BLK)
        total = None
        for blocks, b_ref in ((lower, below), (upper, above)):
            blocks = [block[rows, :] for block in blocks]
            left = jnp.concatenate(blocks, axis=1)
            right = [
                jnp.concatenate(rows_in_order(at_ref, b_ref, (i,), 0), axis=0)
                for i in range(len(groups))
            ]
            right = jnp.concatenate(right, axis=1)
            term = jnp.dot(left, right, preferred_element_type=jnp.float32)
            total = term if total is None else total + term
        here = m == at_ref[0]
        for i in range(len(groups)):
            piece = total[:, i * COL : (i + 1) * COL]
            piece = piece + jnp.where(here, corr_ref[i], 0.0)
            outs[i][rows, :] = piece.astype(outs[i].dtype)


def second_level(groups, at, blocks, below, above, corr):
    return pl.pallas_call(
        functools.partial(second_kernel, groups),
        name="second_level",
        out_shape=tuple(
            jax.ShapeDtypeStruct((M, COL), jnp.bfloat16 if d else jnp.float32)
            for d in groups
        ),
        in_specs=[IN_SMEM] + [IN_VMEM] * 9,
        out_specs=(IN_VMEM,) * len(groups),
        compiler_params=pltpu.CompilerParams(vmem_limit_bytes=24 << 20),
        cost_estimate=pl.CostEstimate(
            flops=4 * BLK * M * len(groups) * COL,
            bytes_accessed=6 << 20,
            transcendentals=0,
        ),
    )(at, *blocks, below, above, corr)


def on_device(right_sides, lower_first, upper_first, lower_second, upper_second):
    rhs = right_sides[0]
    at = jnp.stack([lax.axis_index("y"), lax.axis_index("x")]).astype(jnp.int32)

    def exchanged(value):
        return lax.all_to_all(value, "y", 0, 0, tiled=True)

    firsts = [v[0].reshape(Y, BLK, COL) for v in (lower_first, upper_first)]
    firsts = jnp.stack(firsts, axis=1)
    sent_one = after(rhs, firsts).astype(jnp.bfloat16)
    own = exchanged(firsts)
    near = jnp.stack([moved(sent_one, 1), moved(sent_one, -1)])

    lo_two, up_two = lower_second[0], upper_second[0]
    seconds = after(jnp.stack([lo_two, up_two]), sent_one)
    two_left, two_right = moved(seconds, xs=1), moved(seconds, xs=-1)

    left, right = moved(own, xs=1), moved(own, xs=-1)
    far = moved(left[: Y // 2], xs=1), moved(right[Y // 2 :], xs=-1)
    down, up = moved(near, ys=1), moved(near, ys=-1)
    distant = moved(after(near, down, up), ys=2)
    rhs_rows = exchanged(after(rhs, own, two_left, two_right).reshape(Y, BLK, COL))

    lo_far = moved(after(two_left[0], left), xs=1)
    up_far = moved(after(two_right[1], right), xs=-1)

    blocks = (own, right, *far, left)
    parts = dict(near=near, down=down, up=up)
    parts["far"] = distant
    corr_a, sent_a = first_level(FIRST_GROUPS, at, blocks, parts, rhs_rows)
    late = after(at, sent_a)
    corr_b, sent_b = first_level(LAST_GROUPS, late, blocks, parts, rhs_rows)
    below_a, above_a = moved(sent_a, 2), moved(sent_a, -2)
    below_b, above_b = moved(sent_b, 2), moved(sent_b, -2)
    blocks = (lo_two, up_two, two_left, two_right, lo_far, up_far)
    two, one = second_level(FIRST_GROUPS, at, blocks, below_a, above_a, corr_a)
    late = after(late, two)
    three, total = second_level(LAST_GROUPS, late, blocks, below_b, above_b, corr_b)
    total = total + rhs
    for d, part in ((2, two), (1, one), (3, three)):
        total = total + moved(part, ys=d).astype(jnp.float32)
    return total[None]


def solution(mesh):
    fine = Mesh(mesh.devices.reshape(Z, CORES, Y, X), AXES)
    spec = P(("z", "core"), None, ("y", "x"))
    return jax.shard_map(
        on_device,
        mesh=fine,
        in_specs=(spec,) * 5,
        out_specs=spec,
        check_vma=False,
    )
```

```python
import functools

import jax
import jax.numpy as jnp
from jax import lax
from jax.experimental import pallas as pl
from jax.experimental.pallas import tpu as pltpu
from jax.sharding import Mesh, PartitionSpec as P

Z, CORES, Y, X = 16, 2, 4, 4
PLANES = Z * CORES
M = 2048
BLK = M // Y
COL = 128
AXES = ("z", "core", "y", "x")


def device_index(plane, y, x):
    return (plane * Y + y) * X + x


def moved(value, planes=0, ys=0, xs=0):
    pairs = []
    for plane in range(PLANES):
        if not 0 <= plane + planes < PLANES:
            continue
        for y in range(Y):
            for x in range(X):
                target = device_index(plane + planes, (y + ys) % Y, (x + xs) % X)
                pairs.append((device_index(plane, y, x), target))
    return lax.ppermute(value, AXES, pairs)


def after(value, *before):
    return lax.optimization_barrier((value,) + before)[0]


def rows_in_order(at_ref, ref, index, start):
    starts = [start + lax.rem(at_ref[1] + e, X) * COL for e in range(X)]
    return [ref[index + (pl.ds(pl.multiple_of(at, COL), COL),)] for at in starts]


FIRST_GROUPS, LAST_GROUPS = (2, 1), (3, 0)


def first_kernel(groups, at_ref, *refs):
    own, right_ref, *far, left_ref = refs[: X + 1]
    refs = refs[X + 1 :]
    parts = refs[: 2 * len(groups)]
    rhs_ref, corr_ref, sent_ref = refs[2 * len(groups) :]
    indices = [index for _, index in part_places(groups)]

    total = jnp.zeros((BLK, len(groups) * COL), jnp.float32)
    for k in range(Y):
        for side in (0, 1):
            half, row = divmod(k, Y // 2)
            left = [own[k, side], right_ref[k, side]]
            left += [far[half][row, side], left_ref[k, side]]
            left = jnp.concatenate(left, axis=1)
            right = []
            for part, index in list(zip(parts, indices))[side::2]:
                rows = rows_in_order(at_ref, part, index, k * BLK)
                right.append(jnp.concatenate(rows, axis=0))
            right = jnp.concatenate(right, axis=1)
            total = total + jnp.dot(left, right, preferred_element_type=jnp.float32)

    for i, d in enumerate(groups):
        piece = total[:, i * COL : (i + 1) * COL]
        corr_ref[i] = piece
        owner = lax.rem(at_ref[0] + d, Y)
        sent_ref[i] = (rhs_ref[owner] + piece).astype(jnp.bfloat16)


def part_places(groups):
    places = {
        0: (("near", (0,)), ("near", (1,))),
        1: (("up", (0,)), ("up", (1,))),
        2: (("far", (0,)), ("far", (1,))),
        3: (("down", (0,)), ("down", (1,))),
    }
    return [place for d in groups for place in places[d]]


IN_SMEM = pl.BlockSpec(memory_space=pltpu.SMEM)
IN_VMEM = pl.BlockSpec(memory_space=pltpu.VMEM)


def first_level(groups, at, blocks, parts, rhs):
    count = len(groups)
    parts = [parts[name] for name, _ in part_places(groups)]
    return pl.pallas_call(
        functools.partial(first_kernel, groups),
        name="first_level",
        out_shape=(
            jax.ShapeDtypeStruct((count, BLK, COL), jnp.float32),
            jax.ShapeDtypeStruct((count, BLK, COL), jnp.bfloat16),
        ),
        in_specs=[IN_SMEM] + [IN_VMEM] * (X + len(parts) + 2),
        out_specs=(IN_VMEM, IN_VMEM),
        compiler_params=pltpu.CompilerParams(vmem_limit_bytes=24 << 20),
        cost_estimate=pl.CostEstimate(
            flops=4 * BLK * M * count * COL,
            bytes_accessed=8 << 20,
            transcendentals=0,
        ),
    )(at, *blocks, *parts, rhs)


def second_kernel(groups, at_ref, *refs):
    lo, up, left, right, lo_far, up_far = refs[:6]
    lower = (lo, right.at[0], lo_far, left.at[0])
    upper = (up, right.at[1], up_far, left.at[1])
    below, above, corr_ref, *outs = refs[6:]

    for m in range(Y):
        rows = pl.ds(m * BLK, BLK)
        total = None
        for blocks, b_ref in ((lower, below), (upper, above)):
            blocks = [block[rows, :] for block in blocks]
            left = jnp.concatenate(blocks, axis=1)
            right = [
                jnp.concatenate(rows_in_order(at_ref, b_ref, (i,), 0), axis=0)
                for i in range(len(groups))
            ]
            right = jnp.concatenate(right, axis=1)
            term = jnp.dot(left, right, preferred_element_type=jnp.float32)
            total = term if total is None else total + term
        here = m == at_ref[0]
        for i in range(len(groups)):
            piece = total[:, i * COL : (i + 1) * COL]
            piece = piece + jnp.where(here, corr_ref[i], 0.0)
            outs[i][rows, :] = piece.astype(outs[i].dtype)


def second_level(groups, at, blocks, below, above, corr):
    return pl.pallas_call(
        functools.partial(second_kernel, groups),
        name="second_level",
        out_shape=tuple(
            jax.ShapeDtypeStruct((M, COL), jnp.bfloat16 if d else jnp.float32)
            for d in groups
        ),
        in_specs=[IN_SMEM] + [IN_VMEM] * 9,
        out_specs=(IN_VMEM,) * len(groups),
        compiler_params=pltpu.CompilerParams(vmem_limit_bytes=24 << 20),
        cost_estimate=pl.CostEstimate(
            flops=4 * BLK * M * len(groups) * COL,
            bytes_accessed=6 << 20,
            transcendentals=0,
        ),
    )(at, *blocks, below, above, corr)


def on_device(right_sides, lower_first, upper_first, lower_second, upper_second):
    rhs = right_sides[0]
    at = jnp.stack([lax.axis_index("y"), lax.axis_index("x")]).astype(jnp.int32)

    def exchanged(value):
        return lax.all_to_all(value, "y", 0, 0, tiled=True)

    firsts = [v[0].reshape(Y, BLK, COL) for v in (lower_first, upper_first)]
    firsts = jnp.stack(firsts, axis=1)
    sent_one = rhs.astype(jnp.bfloat16)
    firsts = after(firsts, sent_one)
    own = exchanged(firsts)
    near = jnp.stack([moved(sent_one, 1), moved(sent_one, -1)])

    lo_two, up_two = lower_second[0], upper_second[0]
    seconds = after(jnp.stack([lo_two, up_two]), sent_one)
    two_left, two_right = moved(seconds, xs=1), moved(seconds, xs=-1)

    left, right = moved(own, xs=1), moved(own, xs=-1)
    far = moved(left[: Y // 2], xs=1), moved(right[Y // 2 :], xs=-1)
    down, up = moved(near, ys=1), moved(near, ys=-1)
    distant = moved(after(near, down, up), ys=2)
    rhs_rows = exchanged(after(rhs, own, two_left, two_right).reshape(Y, BLK, COL))

    lo_far = moved(after(two_left[0], left), xs=1)
    up_far = moved(after(two_right[1], right), xs=-1)

    blocks = (own, right, *far, left)
    parts = dict(near=near, down=down, up=up)
    parts["far"] = distant
    corr_a, sent_a = first_level(FIRST_GROUPS, at, blocks, parts, rhs_rows)
    late = after(at, sent_a)
    corr_b, sent_b = first_level(LAST_GROUPS, late, blocks, parts, rhs_rows)
    below_a, above_a = moved(sent_a, 2), moved(sent_a, -2)
    below_b, above_b = moved(sent_b, 2), moved(sent_b, -2)
    blocks = (lo_two, up_two, two_left, two_right, lo_far, up_far)
    two, one = second_level(FIRST_GROUPS, at, blocks, below_a, above_a, corr_a)
    late = after(late, two)
    three, total = second_level(LAST_GROUPS, late, blocks, below_b, above_b, corr_b)
    total = total + rhs
    for d, part in ((2, two), (1, one), (3, three)):
        total = total + moved(part, ys=d).astype(jnp.float32)
    return total[None]


def solution(mesh):
    fine = Mesh(mesh.devices.reshape(Z, CORES, Y, X), AXES)
    spec = P(("z", "core"), None, ("y", "x"))
    return jax.shard_map(
        on_device,
        mesh=fine,
        in_specs=(spec,) * 5,
        out_specs=spec,
        check_vma=False,
    )
```
